256 devices in a mesh: branch: 2 (over y_lo), row: 32 (over z, y_hi, core), seq: 4 (over x).
Axes of the slice: x: 4, y: 4 (y_hi: 2, y_lo: 2; y = y_hi * 2 + y_lo), z: 8, core: 2. Of those that a mesh axis runs over, the one named last changes fastest.
Arguments:
- alignment_input: bfloat16 [256, 256, 256], P('seq', 'row'), may hold values from -6 to 6
- pairwise_input: bfloat16 [128, 256, 256], P('seq', 'row'), may hold values from -30 to 30
- alignment_gain: float32 [256], replicated, may hold values from 0.25 to 1.75
- product_gain: float32 [256], replicated, may hold values from 0.25 to 1.75
- attention_weight: bfloat16 [256, 4, 256], replicated, may hold values from -0.375 to 0.375
- mixing_weight: bfloat16 [256, 256], replicated, may hold values from -0.375 to 0.375
- outer_input_weight: bfloat16 [256, 2, 32], replicated, may hold values from -0.375 to 0.375
- outer_output_weight: bfloat16 [32, 32, 128], replicated, may hold values from -3 to 3
- bias_matrix: bfloat16 [128, 8], replicated, may hold values from -6 to 6
- pairwise_gain: float32 [128], replicated, may hold values from 0.25 to 1.75
- triangle_input_weight: bfloat16 [4, 128, 128], P(None, 'seq'), may hold values from -0.5 to 0.5
- triangle_gate_weight: bfloat16 [128, 128], P('seq'), may hold values from -0.5 to 0.5
- triangle_gain: float32 [128], P('seq'), may hold values from 0.25 to 1.75
- triangle_output_weight: bfloat16 [128, 128], P(None, 'seq'), may hold values from -0.5 to 0.5
- transition_gain: float32 [128], replicated, may hold values from 0.25 to 1.75
- transition_up_weight: bfloat16 [512, 128], P('seq'), may hold values from -0.5 to 0.5
- transition_down_weight: bfloat16 [128, 512], P(None, 'seq'), may hold values from -0.25 to 0.25
Outputs:
- alignment_output: bfloat16 [256, 256, 256], P('seq', 'row', 'branch')
- pairwise_output: bfloat16 [128, 256, 256], P('seq', 'row', 'branch')
The draws below stay inside these ranges and needn't reach their ends.
All inputs are finite; a program needn't handle non-finite values.
Results may differ from the reference program's by a relative error of at most 0.011.
Values may be sent and summed in bfloat16 or wider, within the bound.
A program may use at most 128 MiB of HBM per device.

```python
import jax
import jax.numpy as jnp
from jax import lax

ALIGNMENT_WIDTH = 256
PAIR_WIDTH = 128
ATTENTION_HEADS = 8
HEAD_CHANNELS = 32
PRODUCT_WIDTH = 32
TRI_WIDTH = 128
TRANS_WIDTH = 512
SEQUENCE_COUNT = 256
RESIDUE_COUNT = 256


def bias_values(key):
    inner = jax.random.fold_in(key, 7301)
    draws = jax.random.normal(inner, (PAIR_WIDTH, ATTENTION_HEADS), jnp.float32)
    return jnp.clip(draws * PAIR_WIDTH ** (-0.5), -6.0, 6.0)


def draw_bias_matrix(key, part):
    return bias_values(key).astype(jnp.bfloat16)


def draw_pairwise_input(key, part):
    keys_all = jax.random.split(jax.random.fold_in(key, 4409), 1)
    noise = jax.random.normal(keys_all[0], (PAIR_WIDTH, RESIDUE_COUNT, RESIDUE_COUNT), jnp.float32)
    field = jnp.clip(noise, -6.0, 6.0)
    return field.astype(jnp.bfloat16)


def levels(stream_key, dims, cuts, smallest, largest):
    loudness, own = 1.0, jax.random.fold_in(stream_key, 6)
    for dim, parts in cuts:
        steps = jnp.exp(jax.random.uniform(jax.random.fold_in(own, dim), (parts,), jnp.float32, smallest / len(cuts), largest / len(cuts)))
        loudness = loudness * jnp.repeat(steps, dims[dim] // parts).reshape([-1 if axis == dim else 1 for axis in range(len(dims))])
    return loudness


def gaussian(rng, extent, width, limit, cuts=(), held_as=jnp.bfloat16):
    values = jax.random.normal(rng, extent, jnp.float32) * width
    if len(cuts) > 0:
        values = levels(rng, extent, cuts, -0.22, 0.18) * values
    return jnp.clip(values, min=-limit, max=limit).astype(held_as)


def setup_inputs(seed: int = 0) -> dict:
    seeds = jax.random.split(jax.random.key(seed), 18)
    return {
        "alignment_input": gaussian(seeds[0], (SEQUENCE_COUNT, RESIDUE_COUNT, ALIGNMENT_WIDTH), 1.0, 6.0, ((0, 4), (1, 32))),
        "pairwise_input": draw_pairwise_input(jax.random.fold_in(seeds[17], 71), 0),
        "alignment_gain": jnp.clip(1.0 + 0.15 * jax.random.normal(seeds[2], (ALIGNMENT_WIDTH,), jnp.float32), 0.25, 1.75),
        "product_gain": jnp.clip(1.0 + 0.15 * jax.random.normal(seeds[3], (ALIGNMENT_WIDTH,), jnp.float32), 0.25, 1.75),
        "attention_weight": gaussian(seeds[4], (ALIGNMENT_WIDTH, 4, ATTENTION_HEADS * HEAD_CHANNELS), ALIGNMENT_WIDTH ** -0.5, 0.375),
        "mixing_weight": gaussian(seeds[5], (ATTENTION_HEADS * HEAD_CHANNELS, ALIGNMENT_WIDTH), (ATTENTION_HEADS * HEAD_CHANNELS) ** -0.5, 0.375),
        "outer_input_weight": gaussian(seeds[6], (ALIGNMENT_WIDTH, 2, PRODUCT_WIDTH), ALIGNMENT_WIDTH ** -0.5, 0.375),
        "outer_output_weight": gaussian(seeds[7], (PRODUCT_WIDTH, PRODUCT_WIDTH, PAIR_WIDTH), (max(1, PRODUCT_WIDTH * PRODUCT_WIDTH // SEQUENCE_COUNT)) ** -0.5, 3.0),
        "bias_matrix": draw_bias_matrix(jax.random.fold_in(seeds[17], 71), 0),
        "pairwise_gain": jnp.clip(1.0 + 0.15 * jax.random.normal(seeds[9], (PAIR_WIDTH,), jnp.float32), 0.25, 1.75),
        "triangle_input_weight": gaussian(seeds[10], (4, TRI_WIDTH, PAIR_WIDTH), PAIR_WIDTH ** -0.5, 0.5, ((1, 4),)),
        "triangle_gate_weight": gaussian(seeds[11], (PAIR_WIDTH, PAIR_WIDTH), PAIR_WIDTH ** -0.5, 0.5, ((0, 4),)),
        "triangle_gain": jnp.clip(1.0 + 0.15 * jax.random.normal(seeds[12], (TRI_WIDTH,), jnp.float32), 0.25, 1.75),
        "triangle_output_weight": gaussian(seeds[13], (PAIR_WIDTH, TRI_WIDTH), TRI_WIDTH ** -0.5, 0.5, ((1, 4),)),
        "transition_gain": jnp.clip(1.0 + 0.15 * jax.random.normal(seeds[14], (PAIR_WIDTH,), jnp.float32), 0.25, 1.75),
        "transition_up_weight": gaussian(seeds[15], (TRANS_WIDTH, PAIR_WIDTH), PAIR_WIDTH ** -0.5, 0.5, ((0, 4),)),
        "transition_down_weight": gaussian(seeds[16], (PAIR_WIDTH, TRANS_WIDTH), TRANS_WIDTH ** -0.5, 0.25, ((1, 4),)),
    }


EPSILON = 1e-05

def layer_normalize(values, axis):
    average = lax.optimization_barrier(jnp.mean(values, axis=axis, keepdims=True))
    centred = values - average
    spread = lax.optimization_barrier(jnp.mean(centred * centred, axis=axis, keepdims=True))
    return centred * lax.rsqrt(spread + EPSILON)

def rounded(values):
    return lax.optimization_barrier(values.astype(jnp.bfloat16))

def reference(alignment_input, pairwise_input, alignment_gain, product_gain, attention_weight, mixing_weight, outer_input_weight, outer_output_weight, bias_matrix, pairwise_gain, triangle_input_weight, triangle_gate_weight, triangle_gain, triangle_output_weight, transition_gain, transition_up_weight, transition_down_weight):
    latent_heads = ATTENTION_HEADS * HEAD_CHANNELS
    alignment_single = alignment_input.astype(jnp.float32)
    alignment_module = layer_normalize(alignment_single, 2)
    normalized_values = (alignment_module * alignment_gain).astype(jnp.bfloat16)
    outer_normalized = (alignment_module * product_gain).astype(jnp.bfloat16)
    flattened_rows = normalized_values.reshape(-1, ALIGNMENT_WIDTH)
    outer_input_rows = outer_normalized.reshape(-1, ALIGNMENT_WIDTH)
    projected_values = jnp.dot(flattened_rows, attention_weight.reshape(ALIGNMENT_WIDTH, 4 * latent_heads), preferred_element_type=jnp.float32)
    projected_values = projected_values.reshape(SEQUENCE_COUNT, RESIDUE_COUNT, 4, ATTENTION_HEADS, HEAD_CHANNELS)
    query = rounded(projected_values[:, :, 0] * HEAD_CHANNELS ** (-0.5))
    keys = rounded(projected_values[:, :, 1])
    values = rounded(projected_values[:, :, 2])
    gate = rounded(jax.nn.sigmoid(projected_values[:, :, 3]))
    outer_products = jnp.dot(outer_input_rows, outer_input_weight.reshape(ALIGNMENT_WIDTH, 2 * PRODUCT_WIDTH), preferred_element_type=jnp.float32)
    outer_products = outer_products.astype(jnp.bfloat16).reshape(SEQUENCE_COUNT, RESIDUE_COUNT, 2, PRODUCT_WIDTH)
    left = outer_products[:, :, 0]
    right = outer_products[:, :, 1]
    pair_float = pairwise_input.astype(jnp.float32)
    unit = layer_normalize(pair_float, 0)
    plain = unit.astype(jnp.bfloat16).reshape(PAIR_WIDTH, -1)
    pair_bias = rounded(jnp.dot(bias_matrix.T, plain, preferred_element_type=jnp.float32)).astype(jnp.float32)
    pair_bias = pair_bias.reshape(ATTENTION_HEADS, RESIDUE_COUNT, RESIDUE_COUNT)

    def attend_one(operands):
        query_one, keys_one, values_one, gate_one = operands
        scores = jnp.einsum('ihd,jhd->hij', query_one.astype(jnp.float32), keys_one.astype(jnp.float32), precision=lax.Precision.HIGHEST) + pair_bias
        highest = lax.optimization_barrier(jnp.max(scores, axis=2, keepdims=True))
        weights = jnp.exp(scores - highest)
        totals = lax.optimization_barrier(jnp.sum(weights, axis=2))
        weighted = jnp.einsum('hij,jhd->ihd', rounded(weights).astype(jnp.float32), values_one.astype(jnp.float32), precision=lax.Precision.HIGHEST)
        attended = weighted / jnp.transpose(totals)[:, :, None]
        return (gate_one.astype(jnp.float32) * attended).astype(jnp.bfloat16)
    mixed_heads = lax.map(attend_one, (query, keys, values, gate))
    alignment_output = alignment_single + jnp.dot(mixed_heads.reshape(-1, latent_heads), mixing_weight, preferred_element_type=jnp.float32).reshape(SEQUENCE_COUNT, RESIDUE_COUNT, ALIGNMENT_WIDTH)
    alignment_output = alignment_output.astype(jnp.bfloat16)
    right_matrix = jnp.transpose(right, (0, 2, 1)).reshape(SEQUENCE_COUNT * PRODUCT_WIDTH, RESIDUE_COUNT)

    def outer_row(left_row):
        spread_row = jnp.einsum('sc,cdo->osd', left_row.astype(jnp.float32), outer_output_weight.astype(jnp.float32), precision=lax.Precision.HIGHEST).astype(jnp.bfloat16)
        return jnp.dot(spread_row.reshape(PAIR_WIDTH, -1), right_matrix, preferred_element_type=jnp.float32)
    outer_rows = lax.map(outer_row, jnp.transpose(left, (1, 0, 2)))
    outer_increment = rounded(jnp.transpose(outer_rows, (1, 0, 2)) * (1.0 / SEQUENCE_COUNT)).astype(jnp.float32)
    tri_input = (unit * pairwise_gain[:, None, None]).astype(jnp.bfloat16)
    tri_flat = tri_input.reshape(PAIR_WIDTH, -1)
    linear = jnp.dot(triangle_input_weight.reshape(4 * TRI_WIDTH, PAIR_WIDTH), tri_flat, preferred_element_type=jnp.float32)
    linear = linear.reshape(4, TRI_WIDTH, RESIDUE_COUNT, RESIDUE_COUNT)
    left_tri = rounded(linear[0] * jax.nn.sigmoid(linear[1])).astype(jnp.float32)
    right_tri = rounded(linear[2] * jax.nn.sigmoid(linear[3])).astype(jnp.float32)
    triangle = rounded(jnp.einsum('cik,cjk->cij', left_tri, right_tri, precision=lax.Precision.HIGHEST)).astype(jnp.float32)
    tri_norm = (layer_normalize(triangle, 0) * triangle_gain[:, None, None]).astype(jnp.bfloat16)
    tri_out = jnp.dot(triangle_output_weight, tri_norm.reshape(TRI_WIDTH, -1), preferred_element_type=jnp.float32)
    tri_gate = jax.nn.sigmoid(jnp.dot(triangle_gate_weight, tri_flat, preferred_element_type=jnp.float32))
    first_update = rounded(pair_float + (tri_gate * tri_out).reshape(PAIR_WIDTH, RESIDUE_COUNT, RESIDUE_COUNT)).astype(jnp.float32)
    trans_norm = (layer_normalize(first_update, 0) * transition_gain[:, None, None]).astype(jnp.bfloat16).reshape(PAIR_WIDTH, -1)
    hidden_units = jax.nn.relu(jnp.dot(transition_up_weight, trans_norm, preferred_element_type=jnp.float32)).astype(jnp.bfloat16)
    pair_following = first_update + jnp.dot(transition_down_weight, hidden_units, preferred_element_type=jnp.float32).reshape(PAIR_WIDTH, RESIDUE_COUNT, RESIDUE_COUNT)
    pair_following = rounded(pair_following).astype(jnp.float32)
    pairwise_output = (pair_following + outer_increment).astype(jnp.bfloat16)
    return (alignment_output, pairwise_output)
```

```python
import jax
import jax.numpy as jnp
from jax import lax
from jax.sharding import PartitionSpec as P

EPSILON = 1e-05
BF = jnp.bfloat16
F32 = jnp.float32


def layer_normalize(values, axis):
    average = jnp.mean(values, axis=axis, keepdims=True)
    centred = values - average
    spread = jnp.mean(centred * centred, axis=axis, keepdims=True)
    return centred * lax.rsqrt(spread + EPSILON)


def mm(a, b):
    return jnp.dot(a, b, preferred_element_type=F32)


def shards(
    alignment_input,
    pairwise_input,
    alignment_gain,
    product_gain,
    attention_weight,
    mixing_weight,
    outer_input_weight,
    outer_output_weight,
    bias_matrix,
    pairwise_gain,
    triangle_input_weight,
    triangle_gate_weight,
    triangle_gain,
    triangle_output_weight,
    transition_gain,
    transition_up_weight,
    transition_down_weight,
):
    sl, il, mw = alignment_input.shape
    cl, _, res = pairwise_input.shape
    pw, heads = bias_matrix.shape
    width = mixing_weight.shape[0]
    hd = width // heads
    pc = outer_input_weight.shape[2]
    rows = lax.axis_size("row")
    nq = lax.axis_size("seq")
    nb = lax.axis_size("branch")
    so = sl // rows
    hb = heads // nb
    wb = width // nb
    half = il // nb
    b = lax.axis_index("branch")
    q = lax.axis_index("seq")

    full = lax.all_gather(pairwise_input, "seq", axis=0, tiled=True)
    packed = jnp.concatenate(
        [
            triangle_gate_weight,
            triangle_output_weight.T,
            transition_up_weight,
            transition_down_weight.T,
        ],
        axis=0,
    )
    packed = lax.all_gather(packed, "seq", axis=0)
    tg_full = lax.all_gather(triangle_gain, "seq", axis=0, tiled=True)
    tl = transition_up_weight.shape[0]
    gate_w = packed[:, :cl].reshape(pw, pw)
    out_wt = packed[:, cl : 2 * cl].reshape(pw, pw)
    up_w = packed[:, 2 * cl : 2 * cl + tl].reshape(nq * tl, pw)
    down_wt = packed[:, 2 * cl + tl :].reshape(nq * tl, pw)

    mine = lax.all_to_all(alignment_input, "row", split_axis=0, concat_axis=1, tiled=True)

    unit = layer_normalize(full.astype(F32), 0)
    plain = unit.astype(BF).reshape(pw, -1)
    tri_input = (unit * pairwise_gain[:, None, None]).astype(BF)
    bias_all = lax.dot_general(
        bias_matrix, plain, (((0,), (0,)), ((), ())), preferred_element_type=F32
    ).astype(BF)
    bias_own = lax.dynamic_slice_in_dim(bias_all, hb * b + q, 1, 0).reshape(il, res)
    tri_flat = tri_input.reshape(pw, -1)
    tri_half = lax.dynamic_slice_in_dim(tri_input, half * b, half, 1).reshape(pw, -1)
    lin_l = mm(triangle_input_weight[:2].reshape(2 * cl, pw), tri_half).reshape(2, cl, half, res)
    lin_r = mm(triangle_input_weight[2:].reshape(2 * cl, pw), tri_flat).reshape(2, cl, il, res)
    left_tri = (lin_l[0] * jax.nn.sigmoid(lin_l[1])).astype(BF)
    right_tri = (lin_r[0] * jax.nn.sigmoid(lin_r[1])).astype(BF)
    sent = jnp.concatenate([left_tri, right_tri], axis=1)
    got = lax.all_to_all(sent, "row", split_axis=0, concat_axis=0, tiled=True)
    tri_l = got[:, :half].reshape(rows * half, res)
    tri_r = got[:, half:].reshape(rows * il, res)
    triangle = lax.dot_general(
        tri_l, tri_r, (((1,), (1,)), ((), ())), preferred_element_type=F32
    ).astype(BF)

    bias = lax.all_gather(bias_own, "row", axis=0, tiled=True)
    bias = lax.all_gather(bias, "seq", axis=0)
    stat = layer_normalize(mine.astype(F32), 2)
    normed = (stat * alignment_gain).astype(BF).reshape(so * res, mw)
    weights = lax.dynamic_slice_in_dim(attention_weight, wb * b, wb, 2)
    proj = mm(normed, weights.reshape(mw, 4 * wb)).reshape(so, res, 4, hb, hd)
    query = (proj[:, :, 0] * hd ** (-0.5)).astype(BF)
    keys = proj[:, :, 1].astype(BF)
    values = proj[:, :, 2].astype(BF)
    gate = jax.nn.sigmoid(proj[:, :, 3]).astype(BF)
    scores = jnp.einsum("sihd,sjhd->shij", query, keys, preferred_element_type=F32) + bias.astype(
        F32
    )
    top = jnp.max(scores, axis=3, keepdims=True)
    expo = jnp.exp(scores - top)
    totals = jnp.sum(expo, axis=3)
    weighted = jnp.einsum("shij,sjhd->sihd", expo.astype(BF), values, preferred_element_type=F32)
    mixed = (
        gate.astype(F32) * (weighted / totals.transpose(0, 2, 1)[..., None])
    ).astype(BF)
    mixed = mixed.reshape(so, res, wb)
    mixed = lax.all_to_all(mixed, "row", split_axis=1, concat_axis=0, tiled=True)
    other = lax.ppermute(mixed, "branch", [(i, i ^ 1) for i in range(nb)])
    cols = lax.dynamic_slice_in_dim(mixing_weight, wb * b, wb, 1)
    w_own = lax.dynamic_slice_in_dim(cols, wb * b, wb, 0)
    w_other = lax.dynamic_slice_in_dim(cols, wb * (1 - b), wb, 0)
    residual = lax.dynamic_slice_in_dim(alignment_input, wb * b, wb, 2)
    projected = mm(mixed.reshape(-1, wb), w_own) + mm(other.reshape(-1, wb), w_other)
    alignment_output = (residual.astype(F32) + projected.reshape(sl, il, wb)).astype(BF)

    local = layer_normalize(alignment_input.astype(F32), 2)
    local = (local * product_gain).astype(BF).reshape(-1, mw)
    left = mm(local, outer_input_weight[:, 0]).astype(BF).reshape(sl, il * pc)
    outer_norm = (stat * product_gain).astype(BF)
    right = jnp.einsum(
        "sjm,md->sdj", outer_norm, outer_input_weight[:, 1], preferred_element_type=F32
    ).astype(BF)
    right = lax.dynamic_slice_in_dim(right, (res // nb) * b, res // nb, 2)
    right = lax.all_gather(right, "row", axis=0, tiled=True)
    prod = lax.dot_general(
        left, right.reshape(sl, -1), (((0,), (0,)), ((), ())), preferred_element_type=F32
    ).astype(BF)
    prod = prod.reshape(il, pc, pc, res // nb).transpose(0, 2, 1, 3).reshape(il, pc * pc, res // nb)
    w_outer = outer_output_weight.transpose(1, 0, 2).reshape(pc * pc, pw)
    outer = jnp.einsum("ikj,ko->oij", prod, w_outer, preferred_element_type=F32)
    outer = lax.psum_scatter(outer, "seq", scatter_dimension=0, tiled=True)
    outer_update = (outer * (1.0 / (sl * nq))).astype(BF)

    back = lax.all_to_all(
        triangle.reshape(rows, half, res), "row", split_axis=0, concat_axis=0, tiled=True
    )
    row_tri = lax.all_to_all(back, "seq", split_axis=1, concat_axis=0, tiled=True).reshape(pw, res)
    pick = half * b + q
    pair_row = lax.dynamic_slice_in_dim(full, pick, 1, 1).reshape(pw, res).astype(F32)
    tri_row = lax.dynamic_slice_in_dim(tri_input, pick, 1, 1).reshape(pw, res)
    tri_norm = (layer_normalize(row_tri.astype(F32), 0) * tg_full[:, None]).astype(BF)
    tri_out = lax.dot_general(
        out_wt, tri_norm, (((0,), (0,)), ((), ())), preferred_element_type=F32
    )
    first = (pair_row + jax.nn.sigmoid(mm(gate_w, tri_row)) * tri_out).astype(BF).astype(F32)
    trans = (layer_normalize(first, 0) * transition_gain[:, None]).astype(BF)
    hidden = jax.nn.relu(mm(up_w, trans)).astype(BF)
    pair_next = (
        first
        + lax.dot_general(down_wt, hidden, (((0,), (0,)), ((), ())), preferred_element_type=F32)
    ).astype(BF)
    parts = pair_next.reshape(nq, cl, nb, res // nb).transpose(2, 0, 1, 3)
    parts = parts.reshape(nb * nq, cl, res // nb)
    parts = lax.all_to_all(parts, ("branch", "seq"), split_axis=0, concat_axis=0, tiled=True)
    parts = parts.transpose(1, 0, 2)
    pairwise_output = (parts.astype(F32) + outer_update.astype(F32)).astype(BF)
    return (alignment_output, pairwise_output)


def solution(mesh):
    return jax.shard_map(
        shards,
        mesh=mesh,
        in_specs=(
            P("seq", "row", None),
            P("seq", "row", None),
            P(),
            P(),
            P(),
            P(),
            P(),
            P(),
            P(),
            P(),
            P(None, "seq", None),
            P("seq", None),
            P("seq"),
            P(None, "seq"),
            P(),
            P("seq", None),
            P(None, "seq"),
        ),
        out_specs=(P("seq", "row", "branch"), P("seq", "row", "branch")),
        check_vma=False,
    )
```

```python
import jax
import jax.numpy as jnp
from jax import lax
from jax.sharding import PartitionSpec as P

EPSILON = 1e-05
BF = jnp.bfloat16
F32 = jnp.float32


def layer_normalize(values, axis):
    average = jnp.mean(values, axis=axis, keepdims=True)
    centred = values - average
    spread = jnp.mean(centred * centred, axis=axis, keepdims=True)
    return centred * lax.rsqrt(spread + EPSILON)


def exchange(values, axes):
    return lax.all_to_all(values, axes, split_axis=0, concat_axis=0, tiled=True)


def mm(a, b):
    return jnp.dot(a, b, preferred_element_type=F32)


def shards(
    alignment_input,
    pairwise_input,
    alignment_gain,
    product_gain,
    attention_weight,
    mixing_weight,
    outer_input_weight,
    outer_output_weight,
    bias_matrix,
    pairwise_gain,
    triangle_input_weight,
    triangle_gate_weight,
    triangle_gain,
    triangle_output_weight,
    transition_gain,
    transition_up_weight,
    transition_down_weight,
):
    sl, il, mw = alignment_input.shape
    cl, _, res = pairwise_input.shape
    pw, heads = bias_matrix.shape
    width = mixing_weight.shape[0]
    hd = width // heads
    pc = outer_input_weight.shape[2]
    rows = lax.axis_size("row")
    nq = lax.axis_size("seq")
    nb = lax.axis_size("branch")
    so = sl // rows
    hb = heads // nb
    wb = width // nb
    half = il // nb
    b = lax.axis_index("branch")
    q = lax.axis_index("seq")

    tl = transition_up_weight.shape[0]
    scaled_out = (triangle_output_weight.T.astype(F32) * triangle_gain[:, None]).astype(BF)
    packed = jnp.concatenate(
        [triangle_gate_weight, scaled_out, transition_up_weight, transition_down_weight.T], axis=0
    )
    wide = pairwise_input.reshape(cl * il, res)
    packed = jnp.concatenate(
        [wide[:, : res // 2], wide[:, res // 2 :], packed], axis=0
    )
    everyone = exchange(jnp.broadcast_to(packed[None], (nq,) + packed.shape), "seq")
    n = cl * il
    full = jnp.concatenate([everyone[:, :n], everyone[:, n : 2 * n]], axis=2).reshape(pw, il, res)
    packed = everyone[:, 2 * n :]
    gate_w = packed[:, :cl].reshape(pw, pw)
    out_wt = packed[:, cl : 2 * cl].reshape(pw, pw)
    up_w = packed[:, 2 * cl : 2 * cl + tl].reshape(nq * tl, pw)
    down_wt = packed[:, 2 * cl + tl :].reshape(nq * tl, pw)

    mine = lax.all_to_all(alignment_input, "row", split_axis=0, concat_axis=1, tiled=True)
    stat = layer_normalize(mine.astype(F32), 2)
    normed = (stat * alignment_gain).astype(BF).reshape(so * res, mw)
    outer_norm = (stat * product_gain).astype(BF)
    right = jnp.einsum(
        "sjm,md->dsj", outer_norm, outer_input_weight[:, 1], preferred_element_type=F32
    ).astype(BF)
    hr = res // nb
    right = lax.dynamic_slice_in_dim(right, hr * b, hr, 2).reshape(pc, so * hr)

    unit = layer_normalize(full.astype(F32), 0)
    plain = unit.astype(BF).reshape(pw, -1)
    tri_input = (unit * pairwise_gain[:, None, None]).astype(BF)
    bias_w = lax.dynamic_slice_in_dim(bias_matrix, hb * b, hb, 1)
    bias_own = lax.dot_general(
        bias_w, plain, (((0,), (0,)), ((), ())), preferred_element_type=F32
    ).astype(BF)
    tri_flat = tri_input.reshape(pw, -1)
    tri_half = lax.dynamic_slice_in_dim(tri_input, half * b, half, 1).reshape(pw, -1)
    lin_l = mm(triangle_input_weight[:2].reshape(2 * cl, pw), tri_half).reshape(2, cl, half, res)
    lin_r = mm(triangle_input_weight[2:].reshape(2 * cl, pw), tri_flat).reshape(2, cl, il, res)
    left_tri = (lin_l[0] * jax.nn.sigmoid(lin_l[1])).astype(BF)
    right_tri = (lin_r[0] * jax.nn.sigmoid(lin_r[1])).astype(BF)
    sent = jnp.concatenate(
        [
            jnp.broadcast_to(bias_own.reshape(1, hb * il, res), (rows, hb * il, res)),
            jnp.broadcast_to(right[None], (rows, pc, so * hr)),
            right_tri,
            left_tri,
        ],
        axis=1,
    )
    got = exchange(sent, "row")
    n = hb * il
    bias = got[:, :n].reshape(rows, hb, il, res).transpose(1, 0, 2, 3).reshape(hb, res, res)
    right = got[:, n : n + pc].reshape(rows, pc, so, hr).transpose(1, 0, 2, 3).reshape(pc, sl, hr)
    tri_r = got[:, n + pc : n + pc + il].reshape(rows * il, res)
    tri_l = got[:, n + pc + il :].reshape(rows * half, res)

    triangle = lax.dot_general(
        tri_l, tri_r, (((1,), (1,)), ((), ())), preferred_element_type=F32
    ).astype(BF)
    back = exchange(triangle.reshape(rows, half, res), "row")

    local = layer_normalize(alignment_input.astype(F32), 2)
    local = (local * product_gain).astype(BF).reshape(-1, mw)
    left = mm(local, outer_input_weight[:, 0]).astype(BF).reshape(sl, il * pc)
    prod = jnp.einsum("sk,dsj->kdj", left, right, preferred_element_type=F32).astype(BF)
    prod = prod.reshape(il, pc, pc, hr).transpose(0, 2, 1, 3).reshape(il, pc * pc, hr)
    w_outer = outer_output_weight.transpose(1, 0, 2).reshape(pc * pc, pw)
    outer = jnp.einsum("ikj,ko->oij", prod, w_outer, preferred_element_type=F32)
    outer = (outer * (1.0 / (sl * nq))).astype(BF).reshape(nq, cl * il, hr)

    back = back.transpose(1, 0, 2)
    send = jnp.concatenate([back[:, :, :hr], back[:, :, hr:], outer], axis=1)
    got = exchange(send, "seq")
    row_tri = jnp.concatenate([got[:, :cl], got[:, cl : 2 * cl]], axis=2).reshape(pw, res)
    outer_update = jnp.sum(got[:, 2 * cl :].astype(F32), axis=0).astype(BF).reshape(cl, il, hr)
    pick = half * b + q
    pair_row = lax.dynamic_slice_in_dim(full, pick, 1, 1).reshape(pw, res).astype(F32)
    tri_row = lax.dynamic_slice_in_dim(tri_input, pick, 1, 1).reshape(pw, res)
    tri_norm = layer_normalize(row_tri.astype(F32), 0).astype(BF)
    tri_out = lax.dot_general(
        out_wt, tri_norm, (((0,), (0,)), ((), ())), preferred_element_type=F32
    )
    first = (pair_row + jax.nn.sigmoid(mm(gate_w, tri_row)) * tri_out).astype(BF).astype(F32)
    trans = (layer_normalize(first, 0) * transition_gain[:, None]).astype(BF)
    hidden = jax.nn.relu(mm(up_w, trans)).astype(BF)
    pair_next = (
        first
        + lax.dot_general(down_wt, hidden, (((0,), (0,)), ((), ())), preferred_element_type=F32)
    ).astype(BF)
    parts = pair_next.reshape(nq, cl, nb, hr).transpose(2, 0, 1, 3).reshape(nb * nq, cl, hr)
    parts = exchange(parts, ("branch", "seq")).transpose(1, 0, 2)
    pairwise_output = (parts.astype(F32) + outer_update.astype(F32)).astype(BF)

    weights = lax.dynamic_slice_in_dim(attention_weight, wb * b, wb, 2)
    proj = mm(normed, weights.reshape(mw, 4 * wb)).reshape(so, res, 4, hb, hd)
    query = (proj[:, :, 0] * hd ** (-0.5)).astype(BF)
    keys = proj[:, :, 1].astype(BF)
    values = proj[:, :, 2].astype(BF)
    gate = jax.nn.sigmoid(proj[:, :, 3]).astype(BF)
    scores = jnp.einsum("sihd,sjhd->shij", query, keys, preferred_element_type=F32) + bias.astype(
        F32
    )
    top = jnp.max(scores, axis=3, keepdims=True)
    expo = jnp.exp(scores - top)
    totals = jnp.sum(expo, axis=3)
    weighted = jnp.einsum("shij,sjhd->sihd", expo.astype(BF), values, preferred_element_type=F32)
    mixed = (gate.astype(F32) * (weighted / totals.transpose(0, 2, 1)[..., None])).astype(BF)
    mixed = mixed.reshape(so, rows, il, wb).transpose(1, 0, 2, 3)
    mixed = jnp.broadcast_to(mixed[None], (nb,) + mixed.shape).reshape(nb * rows, so, il, wb)
    mixed = exchange(mixed, ("branch", "row")).reshape(nb, sl * il, wb)
    cols = lax.dynamic_slice_in_dim(mixing_weight, wb * b, wb, 1)
    residual = lax.dynamic_slice_in_dim(alignment_input, wb * b, wb, 2)
    projected = mm(mixed[0], cols[:wb]) + mm(mixed[1], cols[wb:])
    alignment_output = (residual.astype(F32) + projected.reshape(sl, il, wb)).astype(BF)
    return (alignment_output, pairwise_output)


def solution(mesh):
    return jax.shard_map(
        shards,
        mesh=mesh,
        in_specs=(
            P("seq", "row", None),
            P("seq", "row", None),
            P(),
            P(),
            P(),
            P(),
            P(),
            P(),
            P(),
            P(),
            P(None, "seq", None),
            P("seq", None),
            P("seq"),
            P(None, "seq"),
            P(),
            P("seq", None),
            P(None, "seq"),
        ),
        out_specs=(P("seq", "row", "branch"), P("seq", "row", "branch")),
        check_vma=False,
    )
```

```python
import jax
import jax.numpy as jnp
from jax import lax
from jax.experimental import pallas as pl
from jax.experimental.pallas import tpu as pltpu
from jax.sharding import PartitionSpec as P

EPSILON = 1e-05
BF = jnp.bfloat16
F32 = jnp.float32
NZ, NW = 8, 4
NR = NZ * NW
NQ = 4


def mm(a, b):
    return jnp.dot(a, b, preferred_element_type=F32)


def mm_t(a, b):
    return lax.dot_general(a, b, (((1,), (1,)), ((), ())), preferred_element_type=F32)


def normalize(x, axis):
    average = jnp.mean(x, axis=axis, keepdims=True)
    centred = x - average
    spread = jnp.mean(centred * centred, axis=axis, keepdims=True)
    return centred * lax.rsqrt(spread + EPSILON)


def body(
    a_ref,
    p_ref,
    ag_ref,
    pg_ref,
    aw_ref,
    mw_ref,
    ol_ref,
    or_ref,
    oo_ref,
    bm_ref,
    col_ref,
    ti_ref,
    tg_ref,
    tn_ref,
    to_ref,
    up_ref,
    dn_ref,
    msa_ref,
    pair_ref,
    g,
    w,
    tin,
    lt,
    rt,
    ls,
    rs,
    bs,
    lb,
    rb,
    bf,
    mn,
    lx,
    lxt,
    qkv,
    rg,
    rgt,
    pq,
    ob,
    orb,
    tb,
    bk,
    xs,
    xr,
    pn,
    fb,
    mx,
    ao,
    mo,
    ss,
    rv,
):
    b = lax.axis_index("branch")
    r = lax.axis_index("row")
    q = lax.axis_index("seq")
    zi = r // NW
    wi = r % NW
    inside = (r // (NR // 2)) == b
    cols = pl.ds(pl.multiple_of(b * 128, 128), 128)

    def signal(where):
        pl.semaphore_signal(
            barrier, inc=1, device_id=where, device_id_type=pl.DeviceIdType.MESH
        )

    def send(src, dst, k, where):
        pltpu.make_async_remote_copy(
            src_ref=src,
            dst_ref=dst,
            send_sem=ss.at[k],
            recv_sem=rv.at[k],
            device_id=where,
            device_id_type=pl.DeviceIdType.MESH,
        ).start()

    def arrived(view, k):
        pltpu.make_async_copy(view, view, rv.at[k]).wait()

    def left_here(view, k):
        pltpu.make_async_copy(view, view, ss.at[k]).wait()

    def row_peers(do):
        def step(k, carry):
            do(lax.rem(r + k, NR))
            return carry

        lax.fori_loop(1, NR, step, 0)

    barrier = pltpu.get_barrier_semaphore()
    row_peers(lambda peer: signal({"row": peer}))
    for k in range(1, NQ):
        signal({"seq": lax.rem(q + k, NQ)})
    signal({"branch": 1 - b})

    g[q] = jnp.transpose(p_ref[...].astype(F32), (1, 0, 2)).astype(BF)
    w[q, 0:32] = tg_ref[...]
    w[q, 32:160] = jnp.zeros((128, 128), BF)
    w[q, 32:160, 0:32] = (to_ref[...].astype(F32) * tn_ref[...]).astype(BF)
    w[q, 160:288] = up_ref[...]
    w[q, 288:416] = dn_ref[...]
    for s in range(2):
        mn[r, s] = a_ref[s, r]

    pl.semaphore_wait(barrier, NR - 1 + NQ - 1 + 1)

    for k in range(1, NQ):
        send(g.at[q], g.at[q], 0, {"seq": lax.rem(q + k, NQ)})
    row_peers(lambda peer: send(a_ref.at[:, peer], mn.at[r], 1, {"row": peer}))
    for k in range(1, NQ):
        send(w.at[q], w.at[q], 2, {"seq": lax.rem(q + k, NQ)})

    lane = lax.broadcasted_iota(jnp.int32, (16, 8, 256), 2) // 32
    sub = lax.broadcasted_iota(jnp.int32, (16, 8, 256), 1)
    for s in range(2):
        for k in range(2):
            x = a_ref[s, 16 * k : 16 * k + 16].astype(F32).reshape(128, 256)
            x = (normalize(x, 1) * pg_ref[...]).astype(BF)
            x = mm(x, ol_ref[...]).reshape(16, 8, 256)
            lx[32 * s + 16 * k : 32 * s + 16 * k + 16] = jnp.sum(
                jnp.where(lane == sub, x, 0.0), axis=1
            )
    lxt[...] = jnp.transpose(lx[...]).astype(BF)

    arrived(g.at[pl.ds(0, NQ - 1)], 0)
    head = NQ * b + q
    head_row = lax.broadcasted_iota(jnp.int32, (8, 128), 0)
    column = jnp.sum(jnp.where(head_row == head, bm_ref[...], 0.0), axis=0, keepdims=True)

    def pair_row(i, acc):
        unit = normalize(g[:, i].astype(F32).reshape(128, 256), 0)
        pick = jnp.where(head_row == i, column, 0.0).astype(BF)
        acc = acc + mm(pick, unit.astype(BF))
        tri = (unit * col_ref[:, 0:1]).astype(BF)
        tin[i] = tri
        lin = mm(ti_ref[...].reshape(128, 128), tri)
        lt[i] = lin[0:32] * jax.nn.sigmoid(lin[32:64])
        rt[i] = lin[64:96] * jax.nn.sigmoid(lin[96:128])
        return acc

    bs[...] = lax.fori_loop(0, 8, pair_row, jnp.zeros((8, 256), F32)).astype(BF)
    ls[...] = jnp.transpose(lt[...], (1, 0, 2)).astype(BF)
    rs[...] = jnp.transpose(rt[...], (1, 0, 2)).astype(BF)
    lb[r] = ls[r]
    bf[q, r] = bs[...]

    row_peers(lambda peer: send(ls.at[peer], lb.at[r], 3, {"row": peer}))

    @pl.when(inside)
    def _():
        rb[r % (NR // 2)] = rs[r]
        row_peers(lambda peer: send(rs.at[peer], rb.at[r % (NR // 2)], 4, {"row": peer}))

    row_peers(lambda peer: send(bs, bf.at[q, r], 5, {"row": peer}))

    arrived(mn.at[pl.ds(0, NR - 1)], 1)
    for s in range(2):
        x = normalize(mn[:, s].astype(F32).reshape(256, 256), 1)
        normed = (x * ag_ref[...]).astype(BF)
        qkv[s, 0] = (mm(normed, aw_ref[0]) * (32.0**-0.5)).astype(BF)
        qkv[s, 1] = mm(normed, aw_ref[1]).astype(BF)
        qkv[s, 2] = mm(normed, aw_ref[2]).astype(BF)
        qkv[s, 3] = jax.nn.sigmoid(mm(normed, aw_ref[3])).astype(BF)
        right = mm_t(or_ref[...], (x * pg_ref[...]).astype(BF))
        rg[zi, wi, s] = jnp.where(b == 0, right[:, :128], right[:, 128:]).astype(BF)

    def z_peers(k, carry):
        send(rg.at[zi, wi], rg.at[zi, wi], 8, {"row": lax.rem(zi + k, NZ) * NW + wi})
        return carry

    lax.fori_loop(1, NZ, z_peers, 0)

    arrived(lb.at[pl.ds(0, NR - 1)], 3)

    @pl.when(inside)
    def _():
        arrived(rb.at[pl.ds(0, NR // 2 - 1)], 4)

    @pl.when(jnp.logical_not(inside))
    def _():
        arrived(rb, 4)

    tl = lb[...].astype(F32).reshape(256, 256).astype(BF)
    tr = rb[...].astype(F32).reshape(128, 256).astype(BF)
    tb[...] = mm_t(tl, tr).reshape(32, 8, 128).astype(BF)
    bk[r] = tb[r]
    row_peers(lambda peer: send(tb.at[peer], bk.at[r], 6, {"row": peer}))

    arrived(bf.at[0, pl.ds(0, NR - 1)], 5)
    for k in range(1, NQ):
        send(bf.at[q], bf.at[q], 7, {"seq": lax.rem(q + k, NQ)})

    arrived(rg.at[pl.ds(0, NZ - 1), 0], 8)
    for k in range(1, NW):
        send(rg.at[:, wi], rg.at[:, wi], 9, {"row": zi * NW + lax.rem(wi + k, NW)})

    arrived(bk.at[pl.ds(0, NR - 1)], 6)
    xs[...] = jnp.transpose(bk[...].astype(F32), (1, 0, 2)).astype(BF)
    xr[q] = xs[pl.ds(2 * q, 2)]
    for k in range(1, NQ):
        peer = lax.rem(q + k, NQ)
        send(xs.at[pl.ds(2 * peer, 2)], xr.at[q], 10, {"seq": peer})

    arrived(rg.at[:, pl.ds(0, NW - 1)], 9)
    for s in range(2):
        x = rg[:, :, s].astype(F32).reshape(32, 32, 128)
        rgt[:, 32 * s : 32 * s + 32] = jnp.transpose(x, (1, 0, 2)).astype(BF)

    def outer_step(d, carry):
        x = mm(lxt[...], rgt[d]).astype(BF)
        pq[:, pl.ds(pl.multiple_of(d * 32, 32), 32)] = x.reshape(8, 32, 128)
        return carry

    lax.fori_loop(0, 32, outer_step, 0)

    arrived(xr.at[pl.ds(0, NQ - 1)], 10)
    arrived(w.at[pl.ds(0, NQ - 1)], 2)
    row_tri = jnp.concatenate(
        [xr[:, i].astype(F32).reshape(128, 128) for i in range(2)], axis=1
    )
    pair_in = jnp.concatenate(
        [g[:, 2 * q + i, :, cols].astype(F32).reshape(128, 128) for i in range(2)], axis=1
    )
    tri_row = jnp.concatenate([tin[2 * q + i, :, cols] for i in range(2)], axis=1)
    tri_norm = normalize(row_tri, 0).astype(BF)
    tri_out = mm(w[0, 32:160, 0:32], tri_norm[0:32])
    for k in range(1, NQ):
        tri_out = tri_out + mm(w[k, 32:160, 0:32], tri_norm[32 * k : 32 * k + 32])
    gate = jax.nn.sigmoid(mm(w[:, 0:32].reshape(128, 128), tri_row))
    first = (pair_in + gate * tri_out).astype(BF).astype(F32)
    trans = (normalize(first, 0) * col_ref[:, 1:2]).astype(BF)
    moved = first
    for k in range(NQ):
        hidden = jnp.maximum(mm(w[k, 160:288], trans), 0.0).astype(BF)
        moved = moved + mm(w[k, 288:416], hidden)
    moved = moved.astype(BF)
    for i in range(2):
        pn[:, i] = moved[:, 128 * i : 128 * i + 128].reshape(4, 32, 128)
    fb[pl.ds(2 * q, 2)] = pn[q]
    for k in range(1, NQ):
        peer = lax.rem(q + k, NQ)
        send(pn.at[peer], fb.at[pl.ds(2 * q, 2)], 11, {"seq": peer})

    arrived(bf.at[pl.ds(0, NQ - 1)], 7)
    lane_head = lax.broadcasted_iota(jnp.int32, (256, 128), 1) // 32
    for s in range(2):

        def one_head(h, acc):
            here = lane_head == h
            query = jnp.where(here, qkv[s, 0].astype(F32), 0.0).astype(BF)
            score = mm_t(query, qkv[s, 1]) + bf[h].astype(F32).reshape(256, 256)
            expo = jnp.exp(score - jnp.max(score, axis=1, keepdims=True))
            total = jnp.sum(expo, axis=1, keepdims=True)
            value = mm(expo.astype(BF), qkv[s, 2]) / total
            return jnp.where(here, value, acc)

        value = lax.fori_loop(0, 4, one_head, jnp.zeros((256, 128), F32))
        mx[b, s] = (qkv[s, 3].astype(F32) * value).astype(BF)
    send(mx.at[b], mx.at[b], 13, {"branch": 1 - b})

    def project_step(i, carry):
        x = mm(oo_ref[...], pq[i]) * (1.0 / 256.0)
        ob[:, i] = x.astype(BF).reshape(4, 32, 128)
        return carry

    lax.fori_loop(0, 8, project_step, 0)
    orb[q] = ob[q]
    for k in range(1, NQ):
        peer = lax.rem(q + k, NQ)
        send(ob.at[peer], orb.at[q], 12, {"seq": peer})

    arrived(mx.at[0], 13)
    for s in range(2):
        x = mm(mx[0, s], mw_ref[0:128, cols]) + mm(mx[1, s], mw_ref[128:256, cols])
        x = mn[:, s, :, cols].astype(F32).reshape(256, 128) + x
        ao[:, s] = x.reshape(32, 8, 128).astype(BF)
        mo[s, r] = ao[r, s]
    row_peers(lambda peer: send(ao.at[peer], mo.at[:, r], 14, {"row": peer}))

    arrived(fb.at[pl.ds(0, 6)], 11)
    arrived(orb.at[pl.ds(0, NQ - 1)], 12)
    update = orb[0].astype(F32)
    for k in range(1, NQ):
        update = update + orb[k].astype(F32)
    update = update.astype(BF).astype(F32) + fb[...].astype(F32)
    pair_ref[...] = jnp.transpose(update, (1, 0, 2)).astype(BF)

    arrived(mo.at[:, pl.ds(0, NR - 1)], 14)
    msa_ref[...] = mo[...]

    for k, view in (
        (0, g.at[pl.ds(0, NQ - 1)]),
        (1, mn.at[pl.ds(0, NR - 1)]),
        (2, w.at[pl.ds(0, NQ - 1)]),
        (3, lb.at[pl.ds(0, NR - 1)]),
        (5, bf.at[0, pl.ds(0, NR - 1)]),
        (6, bk.at[pl.ds(0, NR - 1)]),
        (7, bf.at[pl.ds(0, NQ - 1)]),
        (8, rg.at[pl.ds(0, NZ - 1), 0]),
        (9, rg.at[:, pl.ds(0, NW - 1)]),
        (10, xr.at[pl.ds(0, NQ - 1)]),
        (11, fb.at[pl.ds(0, 6)]),
        (12, orb.at[pl.ds(0, NQ - 1)]),
        (13, mx.at[0]),
        (14, mo.at[:, pl.ds(0, NR - 1)]),
    ):
        left_here(view, k)

    @pl.when(inside)
    def _():
        left_here(lb.at[pl.ds(0, NR - 1)], 4)


def shards(
    alignment_input,
    pairwise_input,
    alignment_gain,
    product_gain,
    attention_weight,
    mixing_weight,
    outer_input_weight,
    outer_output_weight,
    bias_matrix,
    pairwise_gain,
    triangle_input_weight,
    triangle_gate_weight,
    triangle_gain,
    triangle_output_weight,
    transition_gain,
    transition_up_weight,
    transition_down_weight,
):
    b = lax.axis_index("branch")
    operands = (
        alignment_input.reshape(2, NR, 8, 256),
        pairwise_input,
        alignment_gain.reshape(1, 256),
        product_gain.reshape(1, 256),
        lax.dynamic_slice_in_dim(attention_weight, 128 * b, 128, 2).transpose(1, 0, 2),
        mixing_weight,
        jnp.tile(outer_input_weight[:, 0], (1, 8)),
        outer_input_weight[:, 1].T,
        outer_output_weight.transpose(2, 1, 0).reshape(128, 1024),
        bias_matrix.T.astype(F32),
        jnp.stack([pairwise_gain, transition_gain], axis=1),
        triangle_input_weight,
        triangle_gate_weight,
        triangle_gain.reshape(1, 32),
        triangle_output_weight,
        transition_up_weight,
        transition_down_weight,
    )
    vm = pltpu.VMEM
    msa, pair = pl.pallas_call(
        body,
        out_shape=(
            jax.ShapeDtypeStruct((2, NR, 8, 128), BF),
            jax.ShapeDtypeStruct((32, 8, 128), BF),
        ),
        in_specs=[pl.BlockSpec(memory_space=pltpu.VMEM)] * len(operands),
        out_specs=[pl.BlockSpec(memory_space=pltpu.VMEM)] * 2,
        scratch_shapes=[
            vm((4, 8, 32, 256), BF),
            vm((4, 416, 128), BF),
            vm((8, 128, 256), BF),
            vm((8, 32, 256), F32),
            vm((8, 32, 256), F32),
            vm((32, 8, 256), BF),
            vm((32, 8, 256), BF),
            vm((8, 256), BF),
            vm((32, 8, 256), BF),
            vm((16, 8, 256), BF),
            vm((4, 32, 8, 256), BF),
            vm((32, 2, 8, 256), BF),
            vm((64, 256), F32),
            vm((256, 64), BF),
            vm((2, 4, 256, 128), BF),
            vm((8, 4, 2, 32, 128), BF),
            vm((32, 64, 128), BF),
            vm((8, 1024, 128), BF),
            vm((4, 8, 32, 128), BF),
            vm((4, 8, 32, 128), BF),
            vm((32, 8, 128), BF),
            vm((32, 8, 128), BF),
            vm((8, 32, 128), BF),
            vm((4, 2, 32, 128), BF),
            vm((4, 2, 32, 128), BF),
            vm((8, 32, 128), BF),
            vm((2, 2, 256, 128), BF),
            vm((32, 2, 8, 128), BF),
            vm((2, 32, 8, 128), BF),
            pltpu.SemaphoreType.DMA((15,)),
            pltpu.SemaphoreType.DMA((15,)),
        ],
        compiler_params=pltpu.CompilerParams(
            collective_id=0, has_side_effects=True, vmem_limit_bytes=56 * 2**20
        ),
    )(*operands)
    return msa.reshape(64, 8, 128), pair


def solution(mesh):
    return jax.shard_map(
        shards,
        mesh=mesh,
        in_specs=(
            P("seq", "row", None),
            P("seq", "row", None),
            P(),
            P(),
            P(),
            P(),
            P(),
            P(),
            P(),
            P(),
            P(None, "seq", None),
            P("seq", None),
            P("seq"),
            P(None, "seq"),
            P(),
            P("seq", None),
            P(None, "seq"),
        ),
        out_specs=(P("seq", "row", "branch"), P("seq", "row", "branch")),
        check_vma=False,
    )
```

```python
import jax
import jax.numpy as jnp
from jax import lax
from jax.experimental import pallas as pl
from jax.experimental.pallas import tpu as pltpu
from jax.sharding import PartitionSpec as P

EPSILON = 1e-05
BF = jnp.bfloat16
F32 = jnp.float32
NZ, NW = 8, 4
NR = NZ * NW
NQ = 4


def mm(a, b):
    return jnp.dot(a, b, preferred_element_type=F32)


def mm_t(a, b):
    return lax.dot_general(a, b, (((1,), (1,)), ((), ())), preferred_element_type=F32)


def normalize(x, axis):
    average = jnp.mean(x, axis=axis, keepdims=True)
    centred = x - average
    spread = jnp.mean(centred * centred, axis=axis, keepdims=True)
    return centred * lax.rsqrt(spread + EPSILON)


def column(row):
    n = row.shape[1]
    eye = lax.broadcasted_iota(jnp.int32, (n, n), 0) == lax.broadcasted_iota(
        jnp.int32, (n, n), 1
    )
    return jnp.sum(jnp.where(eye, row, 0.0), axis=1, keepdims=True)


def body(
    a_hbm,
    p_hbm,
    ag_hbm,
    pg_hbm,
    aw_hbm,
    mw_hbm,
    oi_hbm,
    oo_hbm,
    bm_hbm,
    cg_hbm,
    ti_hbm,
    tg_hbm,
    tn_hbm,
    to_hbm,
    cn_hbm,
    up_hbm,
    dn_hbm,
    msa_ref,
    pair_ref,
    a_ref,
    p_ref,
    ag_ref,
    pg_ref,
    aw_ref,
    mw_ref,
    oi_ref,
    oo_ref,
    bm_ref,
    cg_ref,
    ti_ref,
    tg_ref,
    tn_ref,
    to_ref,
    cn_ref,
    up_ref,
    dn_ref,
    awf,
    awt,
    oot,
    g,
    w,
    tin,
    lt,
    rt,
    ls,
    rs,
    bs,
    lb,
    rb,
    bf,
    mn,
    lx,
    lxt,
    qkv,
    rg,
    rgt,
    pq,
    ob,
    orb,
    tb,
    bk,
    xs,
    xr,
    pn,
    fb,
    mx,
    ao,
    mo,
    cs,
    ss,
    rv,
):
    b = lax.axis_index("branch")
    r = lax.axis_index("row")
    q = lax.axis_index("seq")
    zi = r // NW
    wi = r % NW
    inside = (r // (NR // 2)) == b
    cols = pl.ds(pl.multiple_of(b * 128, 128), 128)

    loads = {}
    for n, (src, dst) in enumerate(
        (
            (p_hbm, p_ref),
            (a_hbm, a_ref),
            (tg_hbm, tg_ref),
            (tn_hbm, tn_ref),
            (to_hbm, to_ref),
            (up_hbm, up_ref),
            (dn_hbm, dn_ref),
            (pg_hbm, pg_ref),
            (oi_hbm, oi_ref),
            (aw_hbm.at[:, :, cols], aw_ref),
            (oo_hbm, oo_ref),
            (bm_hbm, bm_ref),
            (cg_hbm, cg_ref),
            (ti_hbm, ti_ref),
            (ag_hbm, ag_ref),
            (cn_hbm, cn_ref),
            (mw_hbm.at[:, cols], mw_ref),
        )
    ):
        loads[n] = pltpu.make_async_copy(src, dst, cs.at[n])
        loads[n].start()

    def signal(where):
        pl.semaphore_signal(
            barrier, inc=1, device_id=where, device_id_type=pl.DeviceIdType.MESH
        )

    def send(src, dst, k, where):
        pltpu.make_async_remote_copy(
            src_ref=src,
            dst_ref=dst,
            send_sem=ss.at[k],
            recv_sem=rv.at[k],
            device_id=where,
            device_id_type=pl.DeviceIdType.MESH,
        ).start()

    def arrived(view, k):
        pltpu.make_async_copy(view, view, rv.at[k]).wait()

    def left_here(view, k):
        pltpu.make_async_copy(view, view, ss.at[k]).wait()

    def row_peers(do):
        def step(k, carry):
            do(lax.rem(r + k, NR))
            return carry

        lax.fori_loop(1, NR, step, 0)

    barrier = pltpu.get_barrier_semaphore()
    row_peers(lambda peer: signal({"row": peer}))
    for k in range(1, NQ):
        signal({"seq": lax.rem(q + k, NQ)})
    signal({"branch": 1 - b})

    loads[0].wait()
    g[q] = jnp.transpose(p_ref[...].astype(F32), (1, 0, 2)).astype(BF)
    loads[1].wait()

    pl.semaphore_wait(barrier, NR - 1 + NQ - 1 + 1)

    for k in range(1, NQ):
        send(g.at[q], g.at[q], 0, {"seq": lax.rem(q + k, NQ)})
    row_peers(lambda peer: send(a_ref.at[:, peer], mn.at[r], 1, {"row": peer}))

    for s in range(2):
        mn[r, s] = a_ref[s, r]
    for n in range(2, 7):
        loads[n].wait()
    w[q, 0:32] = tg_ref[...]
    w[q, 32:64] = (to_ref[...].astype(F32) * column(tn_ref[...])).astype(BF)
    w[q, 64:192] = up_ref[...]
    w[q, 192:320] = dn_ref[...]
    loads[7].wait()
    loads[8].wait()
    lane = lax.broadcasted_iota(jnp.int32, (16, 8, 256), 2) // 32
    sub = lax.broadcasted_iota(jnp.int32, (16, 8, 256), 1)
    wide_left = jnp.concatenate([oi_ref[0]] * 8, axis=0)
    for s in range(2):
        for k in range(2):
            x = a_ref[s, 16 * k : 16 * k + 16].astype(F32).reshape(128, 256)
            x = (normalize(x, 1) * pg_ref[...]).astype(BF)
            x = mm_t(x, wide_left).reshape(16, 8, 256)
            lx[32 * s + 16 * k : 32 * s + 16 * k + 16] = jnp.sum(
                jnp.where(lane == sub, x, 0.0), axis=1
            )
    lxt[...] = jnp.transpose(lx[...]).astype(BF)
    loads[9].wait()
    awf[...] = aw_ref[...].astype(F32).reshape(1024, 128)
    for t in range(4):
        awt[t] = awf[pl.ds(t, 256, stride=4)].astype(BF)
    loads[10].wait()
    x = jnp.transpose(oo_ref[...].astype(F32), (1, 0, 2)).reshape(1024, 128)
    oot[...] = jnp.transpose(x).astype(BF)
    for n in range(11, 17):
        loads[n].wait()

    head_row = lax.broadcasted_iota(jnp.int32, (8, 128), 0)
    pick = jnp.where(head_row == NQ * b + q, bm_ref[...].astype(F32), 0.0)
    pick = jnp.sum(pick, axis=0, keepdims=True)
    pair_gain = column(cg_ref[...])
    arrived(g.at[pl.ds(0, NQ - 1)], 0)

    def bias_row(i, acc):
        unit = normalize(g[:, i].astype(F32).reshape(128, 256), 0)
        tin[i] = (unit * pair_gain).astype(BF)
        return acc + mm(jnp.where(head_row == i, pick, 0.0).astype(BF), unit.astype(BF))

    bs[...] = lax.fori_loop(0, 8, bias_row, jnp.zeros((8, 256), F32)).astype(BF)
    bf[q, r] = bs[...]
    for dz in range(NZ):
        for dw in range(NW):
            if dz or dw:
                peer = lax.rem(zi + dz, NZ) * NW + lax.rem(wi + dw, NW)
                send(bs, bf.at[q, r], 17 + dz, {"row": peer})

    def tri_row_step(i, carry):
        lin = mm(ti_ref[...].reshape(128, 128), tin[i])
        lt[i] = lin[0:32] * jax.nn.sigmoid(lin[32:64])
        rt[i] = lin[64:96] * jax.nn.sigmoid(lin[96:128])
        return carry

    lax.fori_loop(0, 8, tri_row_step, 0)
    ls[...] = jnp.transpose(lt[...], (1, 0, 2)).astype(BF)
    rs[...] = jnp.transpose(rt[...], (1, 0, 2)).astype(BF)
    lb[r] = ls[r]
    row_peers(lambda peer: send(ls.at[peer], lb.at[r], 3, {"row": peer}))

    @pl.when(inside)
    def _():
        rb[r % (NR // 2)] = rs[r]
        row_peers(lambda peer: send(rs.at[peer], rb.at[r % (NR // 2)], 4, {"row": peer}))

    for k in range(1, NQ):
        send(w.at[q], w.at[q], 2, {"seq": lax.rem(q + k, NQ)})

    arrived(mn.at[pl.ds(0, NR - 1)], 1)
    for s in range(2):
        x = normalize(mn[:, s].astype(F32).reshape(256, 256), 1)
        right = mm_t(oi_ref[1], (x * pg_ref[...]).astype(BF))
        rg[zi, wi, s] = jnp.where(b == 0, right[:, :128], right[:, 128:]).astype(BF)
        normed = (x * ag_ref[...]).astype(BF)
        qkv[s, 0] = (mm(normed, awt[0]) * (32.0**-0.5)).astype(BF)
        qkv[s, 1] = mm(normed, awt[1]).astype(BF)
        qkv[s, 2] = mm(normed, awt[2]).astype(BF)
        qkv[s, 3] = jax.nn.sigmoid(mm(normed, awt[3])).astype(BF)

    def z_peers(k, carry):
        send(rg.at[zi, wi], rg.at[zi, wi], 8, {"row": lax.rem(zi + k, NZ) * NW + wi})
        return carry

    lax.fori_loop(1, NZ, z_peers, 0)

    for dz in (0, 1, 7, 2, 6, 3, 5, 4):
        arrived(bf.at[0, pl.ds(0, NW if dz else NW - 1)], 17 + dz)
        part = bf.at[q, pl.ds(lax.rem(zi + NZ - dz, NZ) * NW, NW)]
        for k in range(1, NQ):
            send(part, part, 24 + k, {"seq": lax.rem(q + k, NQ)})

    arrived(lb.at[pl.ds(0, NR - 1)], 3)

    @pl.when(inside)
    def _():
        arrived(rb.at[pl.ds(0, NR // 2 - 1)], 4)

    @pl.when(jnp.logical_not(inside))
    def _():
        arrived(rb, 4)

    tl = lb[...].astype(F32).reshape(256, 256).astype(BF)
    tr = rb[...].astype(F32).reshape(128, 256).astype(BF)
    tb[...] = mm_t(tl, tr).reshape(32, 8, 128).astype(BF)
    bk[r] = tb[r]
    row_peers(lambda peer: send(tb.at[peer], bk.at[r], 6, {"row": peer}))

    arrived(rg.at[pl.ds(0, NZ - 1), 0], 8)
    for k in range(1, NW):
        send(rg.at[:, wi], rg.at[:, wi], 9, {"row": zi * NW + lax.rem(wi + k, NW)})

    lane_head = lax.broadcasted_iota(jnp.int32, (256, 128), 1) // 32
    for s in range(2):
        value = jnp.zeros((256, 128), F32)
        for k in range(NQ):
            h = lax.rem(q + NQ - k, NQ)
            if s == 0 and k:
                arrived(bf.at[0], 24 + k)
            here = lane_head == h
            query = jnp.where(here, qkv[s, 0].astype(F32), 0.0).astype(BF)
            score = mm_t(query, qkv[s, 1]) + bf[h].astype(F32).reshape(256, 256)
            expo = jnp.exp(score - jnp.max(score, axis=1, keepdims=True))
            total = jnp.sum(expo, axis=1, keepdims=True)
            value = jnp.where(here, mm(expo.astype(BF), qkv[s, 2]) / total, value)
        mx[b, s] = (qkv[s, 3].astype(F32) * value).astype(BF)
        send(mx.at[b, s], mx.at[b, s], 13 + s, {"branch": 1 - b})

    arrived(rg.at[:, pl.ds(0, NW - 1)], 9)
    for s in range(2):
        x = rg[:, :, s].astype(F32).reshape(32, 32, 128)
        x = jnp.transpose(x, (1, 0, 2)).astype(BF)
        for d in range(32):
            rgt[32 * s : 32 * s + 32, 128 * d : 128 * d + 128] = x[d]

    def outer_step(n, carry):
        x = mm(lxt[...], rgt[:, pl.ds(pl.multiple_of(n * 256, 256), 256)]).astype(BF)
        for d in range(2):
            for i in range(8):
                pq[
                    i // 2,
                    pl.ds(pl.multiple_of(n * 64 + 32 * d, 32), 32),
                    128 * (i % 2) : 128 * (i % 2) + 128,
                ] = x[32 * i : 32 * i + 32, 128 * d : 128 * d + 128]
        return carry

    lax.fori_loop(0, 16, outer_step, 0)

    arrived(bk.at[pl.ds(0, NR - 1)], 6)
    xs[...] = jnp.transpose(bk[...].astype(F32), (1, 0, 2)).astype(BF)
    xr[q] = xs[pl.ds(2 * q, 2)]
    for k in range(1, NQ):
        peer = lax.rem(q + k, NQ)
        send(xs.at[pl.ds(2 * peer, 2)], xr.at[q], 10, {"seq": peer})

    for s in range(2):
        arrived(mx.at[0, s], 13 + s)
        x = mm(mx[0, s], mw_ref[0:128]) + mm(mx[1, s], mw_ref[128:256])
        x = mn[:, s, :, cols].astype(F32).reshape(256, 128) + x
        ao[:, s] = x.reshape(32, 8, 128).astype(BF)
        mo[s, r] = ao[r, s]
        row_peers(lambda peer: send(ao.at[peer, s], mo.at[s, r], 15 + s, {"row": peer}))

    for n in range(4):
        x = (mm(oot[...], pq[n]) * (1.0 / 256.0)).astype(BF)
        for i in range(2):
            ob[:, 2 * n + i] = x[:, 128 * i : 128 * i + 128].reshape(4, 32, 128)
    orb[q] = ob[q]
    for k in range(1, NQ):
        peer = lax.rem(q + k, NQ)
        send(ob.at[peer], orb.at[q], 12, {"seq": peer})

    arrived(w.at[pl.ds(0, NQ - 1)], 2)
    out_w = w[:, 32:64].astype(F32).reshape(128, 128)
    out_w = jnp.transpose(out_w).astype(BF)
    trans_gain = column(cn_ref[...])
    pair_in = jnp.concatenate(
        [g[:, 2 * q + i, :, cols].astype(F32).reshape(128, 128) for i in range(2)], axis=1
    )
    tri_row = jnp.concatenate([tin[2 * q + i, :, cols] for i in range(2)], axis=1)
    gate = jax.nn.sigmoid(mm(w[:, 0:32].reshape(128, 128), tri_row))
    arrived(xr.at[pl.ds(0, NQ - 1)], 10)
    row_tri = jnp.concatenate(
        [xr[:, i].astype(F32).reshape(128, 128) for i in range(2)], axis=1
    )
    first = pair_in + gate * mm(out_w, normalize(row_tri, 0).astype(BF))
    first = first.astype(BF).astype(F32)
    trans = (normalize(first, 0) * trans_gain).astype(BF)
    moved = first
    for k in range(NQ):
        hidden = jnp.maximum(mm(w[k, 64:192], trans), 0.0).astype(BF)
        moved = moved + mm(w[k, 192:320], hidden)
    moved = moved.astype(BF)
    for i in range(2):
        pn[:, i] = moved[:, 128 * i : 128 * i + 128].reshape(4, 32, 128)
    fb[pl.ds(2 * q, 2)] = pn[q]
    for k in range(1, NQ):
        peer = lax.rem(q + k, NQ)
        send(pn.at[peer], fb.at[pl.ds(2 * q, 2)], 11, {"seq": peer})

    arrived(orb.at[pl.ds(0, NQ - 1)], 12)
    update = orb[0].astype(F32)
    for k in range(1, NQ):
        update = update + orb[k].astype(F32)
    update = update.astype(BF).astype(F32)
    arrived(fb.at[pl.ds(0, 6)], 11)
    update = update + fb[...].astype(F32)
    pair_ref[...] = jnp.transpose(update, (1, 0, 2)).reshape(256, 128).astype(BF)

    for s in range(2):
        arrived(mo.at[s, pl.ds(0, NR - 1)], 15 + s)
        msa_ref[256 * s : 256 * s + 256] = mo[s].astype(F32).reshape(256, 128).astype(BF)

    for k, view in (
        (0, g.at[pl.ds(0, NQ - 1)]),
        (1, mn.at[pl.ds(0, NR - 1)]),
        (2, w.at[pl.ds(0, NQ - 1)]),
        (3, lb.at[pl.ds(0, NR - 1)]),
        (6, bk.at[pl.ds(0, NR - 1)]),
        (8, rg.at[pl.ds(0, NZ - 1), 0]),
        (9, rg.at[:, pl.ds(0, NW - 1)]),
        (10, xr.at[pl.ds(0, NQ - 1)]),
        (11, fb.at[pl.ds(0, 6)]),
        (12, orb.at[pl.ds(0, NQ - 1)]),
        (13, mx.at[0, 0]),
        (14, mx.at[0, 0]),
        (15, mo.at[0, pl.ds(0, NR - 1)]),
        (16, mo.at[0, pl.ds(0, NR - 1)]),
        (17, bf.at[0, pl.ds(0, NW - 1)]),
    ):
        left_here(view, k)
    for dz in range(1, NZ):
        left_here(bf.at[0, pl.ds(0, NW)], 17 + dz)
    for k in range(1, NQ):
        left_here(bf.at[0], 24 + k)

    @pl.when(inside)
    def _():
        left_here(lb.at[pl.ds(0, NR - 1)], 4)


def shards(
    alignment_input,
    pairwise_input,
    alignment_gain,
    product_gain,
    attention_weight,
    mixing_weight,
    outer_input_weight,
    outer_output_weight,
    bias_matrix,
    pairwise_gain,
    triangle_input_weight,
    triangle_gate_weight,
    triangle_gain,
    triangle_output_weight,
    transition_gain,
    transition_up_weight,
    transition_down_weight,
):
    operands = (
        alignment_input.reshape(2, NR, 8, 256),
        pairwise_input,
        alignment_gain.reshape(1, 256),
        product_gain.reshape(1, 256),
        attention_weight,
        mixing_weight,
        outer_input_weight.transpose(1, 2, 0),
        outer_output_weight,
        bias_matrix.T,
        pairwise_gain.reshape(1, 128),
        triangle_input_weight,
        triangle_gate_weight,
        triangle_gain.reshape(1, 32),
        triangle_output_weight.T,
        transition_gain.reshape(1, 128),
        transition_up_weight,
        transition_down_weight,
    )
    vm = pltpu.VMEM
    held = [vm(x.shape, x.dtype) for x in operands]
    held[4] = vm((256, 4, 128), BF)
    held[5] = vm((256, 128), BF)
    msa, pair = pl.pallas_call(
        body,
        out_shape=(
            jax.ShapeDtypeStruct((512, 128), BF),
            jax.ShapeDtypeStruct((256, 128), BF),
        ),
        in_specs=[pl.BlockSpec(memory_space=pltpu.HBM)] * len(operands),
        out_specs=[pl.BlockSpec(memory_space=pltpu.VMEM)] * 2,
        scratch_shapes=held
        + [
            vm((1024, 128), F32),
            vm((4, 256, 128), BF),
            vm((128, 1024), BF),
            vm((4, 8, 32, 256), BF),
            vm((4, 320, 128), BF),
            vm((8, 128, 256), BF),
            vm((8, 32, 256), F32),
            vm((8, 32, 256), F32),
            vm((32, 8, 256), BF),
            vm((32, 8, 256), BF),
            vm((8, 256), BF),
            vm((32, 8, 256), BF),
            vm((16, 8, 256), BF),
            vm((4, 32, 8, 256), BF),
            vm((32, 2, 8, 256), BF),
            vm((64, 256), F32),
            vm((256, 64), BF),
            vm((2, 4, 256, 128), BF),
            vm((8, 4, 2, 32, 128), BF),
            vm((64, 4096), BF),
            vm((4, 1024, 256), BF),
            vm((4, 8, 32, 128), BF),
            vm((4, 8, 32, 128), BF),
            vm((32, 8, 128), BF),
            vm((32, 8, 128), BF),
            vm((8, 32, 128), BF),
            vm((4, 2, 32, 128), BF),
            vm((4, 2, 32, 128), BF),
            vm((8, 32, 128), BF),
            vm((2, 2, 256, 128), BF),
            vm((32, 2, 8, 128), BF),
            vm((2, 32, 8, 128), BF),
            pltpu.SemaphoreType.DMA((17,)),
            pltpu.SemaphoreType.DMA((28,)),
            pltpu.SemaphoreType.DMA((28,)),
        ],
        compiler_params=pltpu.CompilerParams(
            collective_id=0, has_side_effects=True, vmem_limit_bytes=67_043_328
        ),
    )(*operands)
    return msa.reshape(64, 8, 128), pair.reshape(32, 8, 128)


def solution(mesh):
    return jax.shard_map(
        shards,
        mesh=mesh,
        in_specs=(
            P("seq", "row", None),
            P("seq", "row", None),
            P(),
            P(),
            P(),
            P(),
            P(),
            P(),
            P(),
            P(),
            P(None, "seq", None),
            P("seq", None),
            P("seq"),
            P(None, "seq"),
            P(),
            P("seq", None),
            P(None, "seq"),
        ),
        out_specs=(P("seq", "row", "branch"), P("seq", "row", "branch")),
        check_vma=False,
    )
```

```python
import jax
import jax.numpy as jnp
from jax import lax
from jax.experimental import pallas as pl
from jax.experimental.pallas import tpu as pltpu
from jax.sharding import PartitionSpec as P

EPSILON = 1e-05
BF = jnp.bfloat16
F32 = jnp.float32
NZ, NW = 8, 4
NR = NZ * NW
NQ = 4


def mm(a, b):
    return jnp.dot(a, b, preferred_element_type=F32)


def mm_t(a, b):
    return lax.dot_general(a, b, (((1,), (1,)), ((), ())), preferred_element_type=F32)


def normalize(x, axis):
    average = jnp.mean(x, axis=axis, keepdims=True)
    centred = x - average
    spread = jnp.mean(centred * centred, axis=axis, keepdims=True)
    return centred * lax.rsqrt(spread + EPSILON)


def column(row):
    n = row.shape[1]
    eye = lax.broadcasted_iota(jnp.int32, (n, n), 0) == lax.broadcasted_iota(
        jnp.int32, (n, n), 1
    )
    return jnp.sum(jnp.where(eye, row, 0.0), axis=1, keepdims=True)


def body(
    a_hbm,
    p_hbm,
    ag_hbm,
    pg_hbm,
    aw_hbm,
    mw_hbm,
    oi_hbm,
    oo_hbm,
    bm_hbm,
    cg_hbm,
    ti_hbm,
    tg_hbm,
    tn_hbm,
    to_hbm,
    cn_hbm,
    up_hbm,
    dn_hbm,
    msa_ref,
    pair_ref,
    a_ref,
    p_ref,
    ag_ref,
    pg_ref,
    aw_ref,
    mw_ref,
    oi_ref,
    oo_ref,
    bm_ref,
    cg_ref,
    ti_ref,
    tg_ref,
    tn_ref,
    to_ref,
    cn_ref,
    up_ref,
    dn_ref,
    awf,
    awt,
    oot,
    g,
    w,
    tin,
    lt,
    rt,
    ls,
    rs,
    bs,
    lb,
    rb,
    bf,
    mn,
    nm,
    lx,
    lxt,
    qkv,
    rg,
    rgt,
    pq,
    ob,
    orb,
    tb,
    bk,
    xs,
    xr,
    pn,
    fb,
    mx,
    ao,
    mo,
    cs,
    ss,
    rv,
):
    b = lax.axis_index("branch")
    r = lax.axis_index("row")
    q = lax.axis_index("seq")
    zi = r // NW
    wi = r % NW
    inside = (r // (NR // 2)) == b
    cols = pl.ds(pl.multiple_of(b * 128, 128), 128)

    loads = {}
    for n, (src, dst) in enumerate(
        (
            (p_hbm, p_ref),
            (a_hbm, a_ref),
            (tg_hbm, tg_ref),
            (tn_hbm, tn_ref),
            (to_hbm, to_ref),
            (up_hbm, up_ref),
            (dn_hbm, dn_ref),
            (pg_hbm, pg_ref),
            (oi_hbm, oi_ref),
            (aw_hbm.at[:, :, cols], aw_ref),
            (oo_hbm, oo_ref),
            (bm_hbm, bm_ref),
            (cg_hbm, cg_ref),
            (ti_hbm, ti_ref),
            (ag_hbm, ag_ref),
            (cn_hbm, cn_ref),
            (mw_hbm.at[:, cols], mw_ref),
        )
    ):
        loads[n] = pltpu.make_async_copy(src, dst, cs.at[n])
        loads[n].start()

    def signal(where):
        pl.semaphore_signal(
            barrier, inc=1, device_id=where, device_id_type=pl.DeviceIdType.MESH
        )

    def send(src, dst, k, where):
        pltpu.make_async_remote_copy(
            src_ref=src,
            dst_ref=dst,
            send_sem=ss.at[k],
            recv_sem=rv.at[k],
            device_id=where,
            device_id_type=pl.DeviceIdType.MESH,
        ).start()

    def arrived(view, k):
        pltpu.make_async_copy(view, view, rv.at[k]).wait()

    def left_here(view, k):
        pltpu.make_async_copy(view, view, ss.at[k]).wait()

    right_nb = {"seq": lax.rem(q + 1, NQ)}
    left_nb = {"seq": lax.rem(q + NQ - 1, NQ)}
    q_right = lax.rem(q + 1, NQ)
    q_left = lax.rem(q + NQ - 1, NQ)

    def both_ways(view, k):
        for c in range(2):
            send(view(q, c), view(q, c), k + c, right_nb)
            send(view(q, c), view(q, c), k + 2 + c, left_nb)

    def pass_on(view, k):
        arrived(view(q, 0), k)
        send(view(q_left, 0), view(q_left, 0), k + 4, right_nb)
        arrived(view(q, 1), k + 3)
        send(view(q_right, 1), view(q_right, 1), k + 5, left_nb)

    def g_part(slot, c):
        return g.at[slot, pl.ds(4 * c, 4)]

    def w_part(slot, c):
        return w.at[slot, pl.ds(160 * c, 160)]

    def row_peers(do):
        def step(k, carry):
            do(lax.rem(r + k, NR))
            return carry

        lax.fori_loop(1, NR, step, 0)

    barrier = pltpu.get_barrier_semaphore()
    row_peers(lambda peer: signal({"row": peer}))
    for k in range(1, NQ):
        signal({"seq": lax.rem(q + k, NQ)})
    signal({"branch": 1 - b})

    loads[0].wait()
    g[q] = jnp.transpose(p_ref[...].astype(F32), (1, 0, 2)).astype(BF)
    loads[1].wait()

    pl.semaphore_wait(barrier, NR - 1 + NQ - 1 + 1)

    both_ways(g_part, 0)
    row_peers(lambda peer: send(a_ref.at[:, peer], mn.at[r], 12, {"row": peer}))

    for s in range(2):
        mn[r, s] = a_ref[s, r]
    for n in range(2, 7):
        loads[n].wait()
    w[q, 0:32] = tg_ref[...]
    w[q, 32:64] = (to_ref[...].astype(F32) * column(tn_ref[...])).astype(BF)
    w[q, 64:192] = up_ref[...]
    w[q, 192:320] = dn_ref[...]
    pass_on(g_part, 0)
    loads[7].wait()
    loads[8].wait()
    lane = lax.broadcasted_iota(jnp.int32, (16, 8, 256), 2) // 32
    sub = lax.broadcasted_iota(jnp.int32, (16, 8, 256), 1)
    wide_left = jnp.concatenate([oi_ref[0]] * 8, axis=0)
    for s in range(2):
        for k in range(2):
            x = a_ref[s, 16 * k : 16 * k + 16].astype(F32).reshape(128, 256)
            x = (normalize(x, 1) * pg_ref[...]).astype(BF)
            x = mm_t(x, wide_left).reshape(16, 8, 256)
            lx[32 * s + 16 * k : 32 * s + 16 * k + 16] = jnp.sum(
                jnp.where(lane == sub, x, 0.0), axis=1
            )
    lxt[...] = jnp.transpose(lx[...]).astype(BF)
    loads[9].wait()
    awf[...] = aw_ref[...].astype(F32).reshape(1024, 128)
    for t in range(4):
        awt[t] = awf[pl.ds(t, 256, stride=4)].astype(BF)
    loads[10].wait()
    x = jnp.transpose(oo_ref[...].astype(F32), (1, 0, 2)).reshape(1024, 128)
    oot[...] = jnp.transpose(x).astype(BF)
    for n in range(11, 17):
        loads[n].wait()

    head_row = lax.broadcasted_iota(jnp.int32, (8, 128), 0)
    pick = jnp.where(head_row == NQ * b + q, bm_ref[...].astype(F32), 0.0)
    pick = jnp.sum(pick, axis=0, keepdims=True)
    pair_gain = column(cg_ref[...])

    def bias_row(i, acc):
        unit = normalize(g[:, i].astype(F32).reshape(128, 256), 0)
        tin[i] = (unit * pair_gain).astype(BF)
        return acc + mm(jnp.where(head_row == i, pick, 0.0).astype(BF), unit.astype(BF))

    arrived(g_part(q, 0), 2)
    arrived(g_part(q, 0), 4)
    acc = lax.fori_loop(0, 4, bias_row, jnp.zeros((8, 256), F32))
    arrived(g_part(q, 1), 1)
    arrived(g_part(q, 1), 5)
    bs[...] = lax.fori_loop(4, 8, bias_row, acc).astype(BF)
    bf[q, r] = bs[...]
    for dz in range(NZ):
        for dw in range(NW):
            if dz or dw:
                peer = lax.rem(zi + dz, NZ) * NW + lax.rem(wi + dw, NW)
                send(bs, bf.at[q, r], 13 + dz, {"row": peer})
    both_ways(w_part, 6)

    def tri_row_step(i, carry):
        lin = mm(ti_ref[...].reshape(128, 128), tin[i])
        lt[i] = lin[0:32] * jax.nn.sigmoid(lin[32:64])
        rt[i] = lin[64:96] * jax.nn.sigmoid(lin[96:128])
        return carry

    lax.fori_loop(0, 8, tri_row_step, 0)
    ls[...] = jnp.transpose(lt[...], (1, 0, 2)).astype(BF)
    rs[...] = jnp.transpose(rt[...], (1, 0, 2)).astype(BF)
    lb[r] = ls[r]
    row_peers(lambda peer: send(ls.at[peer], lb.at[r], 33, {"row": peer}))

    @pl.when(inside)
    def _():
        rb[r % (NR // 2)] = rs[r]
        row_peers(lambda peer: send(rs.at[peer], rb.at[r % (NR // 2)], 34, {"row": peer}))

    arrived(mn.at[pl.ds(0, NR - 1)], 12)
    for s in range(2):
        x = normalize(mn[:, s].astype(F32).reshape(256, 256), 1)
        right = mm_t(oi_ref[1], (x * pg_ref[...]).astype(BF))
        rg[zi, wi, s] = jnp.where(b == 0, right[:, :128], right[:, 128:]).astype(BF)
        nm[s] = (x * ag_ref[...]).astype(BF)

    def z_peers(k, carry):
        send(rg.at[zi, wi], rg.at[zi, wi], 35, {"row": lax.rem(zi + k, NZ) * NW + wi})
        return carry

    lax.fori_loop(1, NZ, z_peers, 0)
    pass_on(w_part, 6)
    for s in range(2):
        qkv[s, 0] = (mm(nm[s], awt[0]) * (32.0**-0.5)).astype(BF)
        qkv[s, 1] = mm(nm[s], awt[1]).astype(BF)
        qkv[s, 2] = mm(nm[s], awt[2]).astype(BF)
        qkv[s, 3] = jax.nn.sigmoid(mm(nm[s], awt[3])).astype(BF)

    def group(slot, dz):
        return bf.at[slot, pl.ds(lax.rem(zi + NZ - dz, NZ) * NW, NW)]

    for dz in (0, 1, 7, 2, 6, 3, 5, 4):
        arrived(bf.at[0, pl.ds(0, NW if dz else NW - 1)], 13 + dz)
        part = group(q, dz)
        send(part, part, 21 + dz if dz < 4 else 25, right_nb)
        send(part, part, 33 - dz if dz >= 4 else 30, left_nb)
    for n in range(4):
        arrived(bf.at[0, pl.ds(0, NW)], 21 + n)
        send(group(q_left, n), group(q_left, n), 31, right_nb)
        arrived(bf.at[0, pl.ds(0, NW)], 26 + n)
        send(group(q_right, 7 - n), group(q_right, 7 - n), 32, left_nb)

    arrived(rg.at[pl.ds(0, NZ - 1), 0], 35)
    w_core = wi + 1 - 2 * (wi % 2)
    w_far = lax.rem(wi + 2, NW)
    other_core = {"row": zi * NW + w_core}
    send(rg.at[:, wi], rg.at[:, wi], 37, {"row": zi * NW + w_far})
    send(rg.at[:, wi], rg.at[:, wi], 36, other_core)

    arrived(lb.at[pl.ds(0, NR - 1)], 33)

    @pl.when(inside)
    def _():
        arrived(rb.at[pl.ds(0, NR // 2 - 1)], 34)

    @pl.when(jnp.logical_not(inside))
    def _():
        arrived(rb, 34)

    tl = lb[...].astype(F32).reshape(256, 256).astype(BF)
    tr = rb[...].astype(F32).reshape(128, 256).astype(BF)
    tb[...] = mm_t(tl, tr).reshape(32, 8, 128).astype(BF)
    bk[r] = tb[r]
    row_peers(lambda peer: send(tb.at[peer], bk.at[r], 39, {"row": peer}))

    lane_head = lax.broadcasted_iota(jnp.int32, (256, 128), 1) // 32
    for s in range(2):
        value = jnp.zeros((256, 128), F32)
        for k in range(NQ):
            h = lax.rem(q + (0, 1, 3, 2)[k], NQ)
            if s == 0 and k == 1:
                arrived(bf.at[0, pl.ds(0, 4 * NW)], 30)
            if s == 0 and k == 2:
                arrived(bf.at[0, pl.ds(0, 4 * NW)], 25)
            if s == 0 and k == 3:
                arrived(bf.at[0, pl.ds(0, 4 * NW)], 31)
                arrived(bf.at[0, pl.ds(0, 4 * NW)], 32)
            here = lane_head == h
            query = jnp.where(here, qkv[s, 0].astype(F32), 0.0).astype(BF)
            score = mm_t(query, qkv[s, 1]) + bf[h].astype(F32).reshape(256, 256)
            expo = jnp.exp(score - jnp.max(score, axis=1, keepdims=True))
            total = jnp.sum(expo, axis=1, keepdims=True)
            value = jnp.where(here, mm(expo.astype(BF), qkv[s, 2]) / total, value)
        mx[b, s] = (qkv[s, 3].astype(F32) * value).astype(BF)
        send(mx.at[b, s], mx.at[b, s], 43 + s, {"branch": 1 - b})

    arrived(rg.at[:, 0], 37)
    send(rg.at[:, w_far], rg.at[:, w_far], 38, other_core)

    for s in range(2):
        arrived(mx.at[0, s], 43 + s)
        x = mm(mx[0, s], mw_ref[0:128]) + mm(mx[1, s], mw_ref[128:256])
        x = mn[:, s, :, cols].astype(F32).reshape(256, 128) + x
        ao[:, s] = x.reshape(32, 8, 128).astype(BF)
        mo[s, r] = ao[r, s]
        row_peers(lambda peer: send(ao.at[peer, s], mo.at[s, r], 45 + s, {"row": peer}))

    arrived(rg.at[:, 0], 36)
    arrived(rg.at[:, 0], 38)
    for s in range(2):
        x = rg[:, :, s].astype(F32).reshape(32, 32, 128)
        x = jnp.transpose(x, (1, 0, 2)).astype(BF)
        for d in range(32):
            rgt[32 * s : 32 * s + 32, 128 * d : 128 * d + 128] = x[d]

    def outer_step(n, carry):
        x = mm(lxt[...], rgt[:, pl.ds(pl.multiple_of(n * 256, 256), 256)]).astype(BF)
        for d in range(2):
            for i in range(8):
                pq[
                    i // 2,
                    pl.ds(pl.multiple_of(n * 64 + 32 * d, 32), 32),
                    128 * (i % 2) : 128 * (i % 2) + 128,
                ] = x[32 * i : 32 * i + 32, 128 * d : 128 * d + 128]
        return carry

    lax.fori_loop(0, 16, outer_step, 0)

    arrived(bk.at[pl.ds(0, NR - 1)], 39)
    xs[...] = jnp.transpose(bk[...].astype(F32), (1, 0, 2)).astype(BF)
    xr[q] = xs[pl.ds(2 * q, 2)]
    for k in range(1, NQ):
        peer = lax.rem(q + k, NQ)
        send(xs.at[pl.ds(2 * peer, 2)], xr.at[q], 40, {"seq": peer})

    for n in range(4):
        x = (mm(oot[...], pq[n]) * (1.0 / 256.0)).astype(BF)
        for i in range(2):
            ob[:, 2 * n + i] = x[:, 128 * i : 128 * i + 128].reshape(4, 32, 128)
    orb[q] = ob[q]
    for k in range(1, NQ):
        peer = lax.rem(q + k, NQ)
        send(ob.at[peer], orb.at[q], 42, {"seq": peer})

    for k, c in ((7, 1), (8, 0), (10, 0), (11, 1)):
        arrived(w_part(q, c), k)
    out_w = w[:, 32:64].astype(F32).reshape(128, 128)
    out_w = jnp.transpose(out_w).astype(BF)
    trans_gain = column(cn_ref[...])
    pair_in = jnp.concatenate(
        [g[:, 2 * q + i, :, cols].astype(F32).reshape(128, 128) for i in range(2)], axis=1
    )
    tri_row = jnp.concatenate([tin[2 * q + i, :, cols] for i in range(2)], axis=1)
    gate = jax.nn.sigmoid(mm(w[:, 0:32].reshape(128, 128), tri_row))
    arrived(xr.at[pl.ds(0, NQ - 1)], 40)
    row_tri = jnp.concatenate(
        [xr[:, i].astype(F32).reshape(128, 128) for i in range(2)], axis=1
    )
    first = pair_in + gate * mm(out_w, normalize(row_tri, 0).astype(BF))
    first = first.astype(BF).astype(F32)
    trans = (normalize(first, 0) * trans_gain).astype(BF)
    moved = first
    for k in range(NQ):
        hidden = jnp.maximum(mm(w[k, 64:192], trans), 0.0).astype(BF)
        moved = moved + mm(w[k, 192:320], hidden)
    moved = moved.astype(BF)
    for i in range(2):
        pn[:, i] = moved[:, 128 * i : 128 * i + 128].reshape(4, 32, 128)
    fb[pl.ds(2 * q, 2)] = pn[q]
    for k in range(1, NQ):
        peer = lax.rem(q + k, NQ)
        send(pn.at[peer], fb.at[pl.ds(2 * q, 2)], 41, {"seq": peer})

    arrived(orb.at[pl.ds(0, NQ - 1)], 42)
    update = orb[0].astype(F32)
    for k in range(1, NQ):
        update = update + orb[k].astype(F32)
    update = update.astype(BF).astype(F32)
    arrived(fb.at[pl.ds(0, 6)], 41)
    update = update + fb[...].astype(F32)
    pair_ref[...] = jnp.transpose(update, (1, 0, 2)).reshape(256, 128).astype(BF)

    for s in range(2):
        arrived(mo.at[s, pl.ds(0, NR - 1)], 45 + s)
        msa_ref[256 * s : 256 * s + 256] = mo[s].astype(F32).reshape(256, 128).astype(BF)

    for c in range(2):
        for k in (0, 2, 4):
            left_here(g_part(q, c), k + c)
            left_here(w_part(q, c), 6 + k + c)
    for n in range(8):
        left_here(bf.at[0, pl.ds(0, NW if n else NW - 1)], 13 + n)
    for n in range(4):
        left_here(bf.at[0, pl.ds(0, NW)], 21 + n)
        left_here(bf.at[0, pl.ds(0, NW)], 26 + n)
    for k in (25, 30, 31, 32):
        left_here(bf.at[0, pl.ds(0, 4 * NW)], k)
    for k, view in (
        (12, mn.at[pl.ds(0, NR - 1)]),
        (33, lb.at[pl.ds(0, NR - 1)]),
        (35, rg.at[pl.ds(0, NZ - 1), 0]),
        (36, rg.at[:, 0]),
        (37, rg.at[:, 0]),
        (38, rg.at[:, 0]),
        (39, bk.at[pl.ds(0, NR - 1)]),
        (40, xr.at[pl.ds(0, NQ - 1)]),
        (41, fb.at[pl.ds(0, 6)]),
        (42, orb.at[pl.ds(0, NQ - 1)]),
        (43, mx.at[0, 0]),
        (44, mx.at[0, 0]),
        (45, mo.at[0, pl.ds(0, NR - 1)]),
        (46, mo.at[0, pl.ds(0, NR - 1)]),
    ):
        left_here(view, k)

    @pl.when(inside)
    def _():
        left_here(lb.at[pl.ds(0, NR - 1)], 34)


def hand_over(msa_in, pair_in, msa_out, pair_out):
    msa_out[...] = msa_in[...]
    pair_out[...] = pair_in[...]


def shards(
    alignment_input,
    pairwise_input,
    alignment_gain,
    product_gain,
    attention_weight,
    mixing_weight,
    outer_input_weight,
    outer_output_weight,
    bias_matrix,
    pairwise_gain,
    triangle_input_weight,
    triangle_gate_weight,
    triangle_gain,
    triangle_output_weight,
    transition_gain,
    transition_up_weight,
    transition_down_weight,
):
    operands = (
        alignment_input.reshape(2, NR, 8, 256),
        pairwise_input,
        alignment_gain.reshape(1, 256),
        product_gain.reshape(1, 256),
        attention_weight,
        mixing_weight,
        outer_input_weight.transpose(1, 2, 0),
        outer_output_weight,
        bias_matrix.T,
        pairwise_gain.reshape(1, 128),
        triangle_input_weight,
        triangle_gate_weight,
        triangle_gain.reshape(1, 32),
        triangle_output_weight.T,
        transition_gain.reshape(1, 128),
        transition_up_weight,
        transition_down_weight,
    )
    vm = pltpu.VMEM
    held = [vm(x.shape, x.dtype) for x in operands]
    held[4] = vm((256, 4, 128), BF)
    held[5] = vm((256, 128), BF)
    msa, pair = pl.pallas_call(
        body,
        out_shape=(
            jax.ShapeDtypeStruct((512, 128), BF),
            jax.ShapeDtypeStruct((256, 128), BF),
        ),
        in_specs=[pl.BlockSpec(memory_space=pltpu.HBM)] * len(operands),
        out_specs=[pl.BlockSpec(memory_space=pltpu.VMEM)] * 2,
        scratch_shapes=held
        + [
            vm((1024, 128), F32),
            vm((4, 256, 128), BF),
            vm((128, 1024), BF),
            vm((4, 8, 32, 256), BF),
            vm((4, 320, 128), BF),
            vm((8, 128, 256), BF),
            vm((8, 32, 256), F32),
            vm((8, 32, 256), F32),
            vm((32, 8, 256), BF),
            vm((32, 8, 256), BF),
            vm((8, 256), BF),
            vm((32, 8, 256), BF),
            vm((16, 8, 256), BF),
            vm((4, 32, 8, 256), BF),
            vm((32, 2, 8, 256), BF),
            vm((2, 256, 256), BF),
            vm((64, 256), F32),
            vm((256, 64), BF),
            vm((2, 4, 256, 128), BF),
            vm((8, 4, 2, 32, 128), BF),
            vm((64, 4096), BF),
            vm((4, 1024, 256), BF),
            vm((4, 8, 32, 128), BF),
            vm((4, 8, 32, 128), BF),
            vm((32, 8, 128), BF),
            vm((32, 8, 128), BF),
            vm((8, 32, 128), BF),
            vm((4, 2, 32, 128), BF),
            vm((4, 2, 32, 128), BF),
            vm((8, 32, 128), BF),
            vm((2, 2, 256, 128), BF),
            vm((32, 2, 8, 128), BF),
            vm((2, 32, 8, 128), BF),
            pltpu.SemaphoreType.DMA((17,)),
            pltpu.SemaphoreType.DMA((47,)),
            pltpu.SemaphoreType.DMA((47,)),
        ],
        compiler_params=pltpu.CompilerParams(
            collective_id=0, has_side_effects=True, vmem_limit_bytes=67_043_328
        ),
    )(*operands)
    msa, pair = pl.pallas_call(
        hand_over,
        out_shape=(
            jax.ShapeDtypeStruct((512, 128), BF),
            jax.ShapeDtypeStruct((256, 128), BF),
        ),
        in_specs=[pl.BlockSpec(memory_space=pltpu.VMEM)] * 2,
        out_specs=[pl.BlockSpec(memory_space=pltpu.VMEM)] * 2,
    )(msa, pair)
    return msa.reshape(64, 8, 128), pair.reshape(32, 8, 128)


def solution(mesh):
    return jax.shard_map(
        shards,
        mesh=mesh,
        in_specs=(
            P("seq", "row", None),
            P("seq", "row", None),
            P(),
            P(),
            P(),
            P(),
            P(),
            P(),
            P(),
            P(),
            P(None, "seq", None),
            P("seq", None),
            P("seq"),
            P(None, "seq"),
            P(),
            P("seq", None),
            P(None, "seq"),
        ),
        out_specs=(P("seq", "row", "branch"), P("seq", "row", "branch")),
        check_vma=False,
    )
```

```python
import jax
import jax.numpy as jnp
from jax import lax
from jax.experimental import pallas as pl
from jax.experimental.pallas import tpu as pltpu
from jax.sharding import PartitionSpec as P

EPSILON = 1e-05
BF = jnp.bfloat16
F32 = jnp.float32
NZ, NW = 8, 4
NR = NZ * NW
NQ = 4


def mm(a, b):
    return jnp.dot(a, b, preferred_element_type=F32)


def mm_t(a, b):
    return lax.dot_general(a, b, (((1,), (1,)), ((), ())), preferred_element_type=F32)


def normalize(x, axis):
    average = jnp.mean(x, axis=axis, keepdims=True)
    centred = x - average
    spread = jnp.mean(centred * centred, axis=axis, keepdims=True)
    return centred * lax.rsqrt(spread + EPSILON)


def column(row):
    n = row.shape[1]
    eye = lax.broadcasted_iota(jnp.int32, (n, n), 0) == lax.broadcasted_iota(
        jnp.int32, (n, n), 1
    )
    return jnp.sum(jnp.where(eye, row, 0.0), axis=1, keepdims=True)


def body(
    a_hbm,
    p_hbm,
    ag_hbm,
    pg_hbm,
    aw_hbm,
    mw_hbm,
    oi_hbm,
    oo_hbm,
    bm_hbm,
    cg_hbm,
    ti_hbm,
    tg_hbm,
    tn_hbm,
    to_hbm,
    cn_hbm,
    up_hbm,
    dn_hbm,
    msa_ref,
    pair_ref,
    a_ref,
    p_ref,
    ag_ref,
    pg_ref,
    aw_ref,
    mw_ref,
    oi_ref,
    oo_ref,
    bm_ref,
    cg_ref,
    ti_ref,
    tg_ref,
    tn_ref,
    to_ref,
    cn_ref,
    up_ref,
    dn_ref,
    awf,
    awt,
    oot,
    g,
    w,
    tin,
    lt,
    rt,
    ls,
    rs,
    bs,
    lb,
    rb,
    bf,
    mn,
    nm,
    lx,
    lxt,
    qkv,
    rg,
    rgt,
    pq,
    ob,
    orb,
    tb,
    bk,
    xs,
    xr,
    pn,
    fb,
    mx,
    ao,
    mo,
    cs,
    ss,
    rv,
):
    b = lax.axis_index("branch")
    r = lax.axis_index("row")
    q = lax.axis_index("seq")
    zi = r // NW
    wi = r % NW
    inside = (r // (NR // 2)) == b
    cols = pl.ds(pl.multiple_of(b * 128, 128), 128)

    loads = {}
    for n, (src, dst) in enumerate(
        (
            (p_hbm, p_ref),
            (a_hbm, a_ref),
            (tg_hbm, tg_ref),
            (tn_hbm, tn_ref),
            (to_hbm, to_ref),
            (up_hbm, up_ref),
            (dn_hbm, dn_ref),
            (pg_hbm, pg_ref),
            (oi_hbm, oi_ref),
            (aw_hbm.at[:, :, cols], aw_ref),
            (oo_hbm, oo_ref),
            (bm_hbm, bm_ref),
            (cg_hbm, cg_ref),
            (ti_hbm, ti_ref),
            (ag_hbm, ag_ref),
            (cn_hbm, cn_ref),
            (mw_hbm.at[:, cols], mw_ref),
        )
    ):
        loads[n] = pltpu.make_async_copy(src, dst, cs.at[n])
        loads[n].start()

    def signal(where):
        pl.semaphore_signal(
            barrier, inc=1, device_id=where, device_id_type=pl.DeviceIdType.MESH
        )

    def send(src, dst, k, where):
        pltpu.make_async_remote_copy(
            src_ref=src,
            dst_ref=dst,
            send_sem=ss.at[k],
            recv_sem=rv.at[k],
            device_id=where,
            device_id_type=pl.DeviceIdType.MESH,
        ).start()

    def arrived(view, k):
        pltpu.make_async_copy(view, view, rv.at[k]).wait()

    def left_here(view, k):
        pltpu.make_async_copy(view, view, ss.at[k]).wait()

    right_nb = {"seq": lax.rem(q + 1, NQ)}
    left_nb = {"seq": lax.rem(q + NQ - 1, NQ)}
    q_right = lax.rem(q + 1, NQ)
    q_left = lax.rem(q + NQ - 1, NQ)

    def both_ways(view, k):
        for c in range(2):
            send(view(q, c), view(q, c), k + c, right_nb)
            send(view(q, c), view(q, c), k + 2 + c, left_nb)

    def pass_on(view, k):
        arrived(view(q, 0), k)
        send(view(q_left, 0), view(q_left, 0), k + 4, right_nb)
        arrived(view(q, 1), k + 3)
        send(view(q_right, 1), view(q_right, 1), k + 5, left_nb)

    def g_part(slot, c):
        return g.at[slot, pl.ds(4 * c, 4)]

    def w_part(slot, c):
        return w.at[slot, pl.ds(160 * c, 160)]

    def row_peers(do):
        def step(k, carry):
            do(lax.rem(r + k, NR))
            return carry

        lax.fori_loop(1, NR, step, 0)

    barrier = pltpu.get_barrier_semaphore()
    row_peers(lambda peer: signal({"row": peer}))
    for k in range(1, NQ):
        signal({"seq": lax.rem(q + k, NQ)})
    signal({"branch": 1 - b})

    loads[0].wait()
    g[q] = jnp.transpose(p_ref[...].astype(F32), (1, 0, 2)).astype(BF)
    loads[1].wait()

    pl.semaphore_wait(barrier, NR - 1 + NQ - 1 + 1)

    both_ways(g_part, 0)
    row_peers(lambda peer: send(a_ref.at[:, peer], mn.at[r], 12, {"row": peer}))

    for s in range(2):
        mn[r, s] = a_ref[s, r]
    for n in range(2, 7):
        loads[n].wait()
    w[q, 0:32] = tg_ref[...]
    w[q, 32:64] = (to_ref[...].astype(F32) * column(tn_ref[...])).astype(BF)
    w[q, 64:192] = up_ref[...]
    w[q, 192:320] = dn_ref[...]
    pass_on(g_part, 0)
    loads[7].wait()
    loads[8].wait()
    lane = lax.broadcasted_iota(jnp.int32, (16, 8, 256), 2) // 32
    sub = lax.broadcasted_iota(jnp.int32, (16, 8, 256), 1)
    wide_left = jnp.concatenate([oi_ref[0]] * 8, axis=0)
    for s in range(2):
        for k in range(2):
            x = a_ref[s, 16 * k : 16 * k + 16].astype(F32).reshape(128, 256)
            x = (normalize(x, 1) * pg_ref[...]).astype(BF)
            x = mm_t(x, wide_left).reshape(16, 8, 256)
            lx[32 * s + 16 * k : 32 * s + 16 * k + 16] = jnp.sum(
                jnp.where(lane == sub, x, 0.0), axis=1
            )
    lxt[...] = jnp.transpose(lx[...]).astype(BF)
    loads[9].wait()
    awf[...] = aw_ref[...].astype(F32).reshape(1024, 128)
    for t in range(4):
        awt[t] = awf[pl.ds(t, 256, stride=4)].astype(BF)
    loads[10].wait()
    x = jnp.transpose(oo_ref[...].astype(F32), (1, 0, 2)).reshape(1024, 128)
    oot[...] = jnp.transpose(x).astype(BF)
    for n in range(11, 17):
        loads[n].wait()

    head_row = lax.broadcasted_iota(jnp.int32, (8, 128), 0)
    pick = jnp.where(head_row == NQ * b + q, bm_ref[...].astype(F32), 0.0)
    pick = jnp.sum(pick, axis=0, keepdims=True)
    pair_gain = column(cg_ref[...])

    def bias_row(i, acc):
        unit = normalize(g[:, i].astype(F32).reshape(128, 256), 0)
        tin[i] = (unit * pair_gain).astype(BF)
        return acc + mm(jnp.where(head_row == i, pick, 0.0).astype(BF), unit.astype(BF))

    arrived(g_part(q, 0), 2)
    arrived(g_part(q, 0), 4)
    acc = lax.fori_loop(0, 4, bias_row, jnp.zeros((8, 256), F32), unroll=4)
    arrived(g_part(q, 1), 1)
    arrived(g_part(q, 1), 5)
    bs[...] = lax.fori_loop(4, 8, bias_row, acc, unroll=4).astype(BF)
    bf[q, r] = bs[...]
    for dz in range(NZ):
        for dw in range(NW):
            if dz or dw:
                peer = lax.rem(zi + dz, NZ) * NW + lax.rem(wi + dw, NW)
                send(bs, bf.at[q, r], 13 + dz, {"row": peer})
    both_ways(w_part, 6)

    def tri_row_step(i, carry):
        lin = mm(ti_ref[...].reshape(128, 128), tin[i])
        lt[i] = lin[0:32] * jax.nn.sigmoid(lin[32:64])
        rt[i] = lin[64:96] * jax.nn.sigmoid(lin[96:128])
        return carry

    lax.fori_loop(0, 8, tri_row_step, 0, unroll=4)
    ls[...] = jnp.transpose(lt[...], (1, 0, 2)).astype(BF)
    rs[...] = jnp.transpose(rt[...], (1, 0, 2)).astype(BF)
    lb[r] = ls[r]
    row_peers(lambda peer: send(ls.at[peer], lb.at[r], 33, {"row": peer}))

    @pl.when(inside)
    def _():
        rb[r % (NR // 2)] = rs[r]
        row_peers(lambda peer: send(rs.at[peer], rb.at[r % (NR // 2)], 34, {"row": peer}))

    arrived(mn.at[pl.ds(0, NR - 1)], 12)
    for s in range(2):
        x = normalize(mn[:, s].astype(F32).reshape(256, 256), 1)
        right = mm_t(oi_ref[1], (x * pg_ref[...]).astype(BF))
        rg[zi, wi, s] = jnp.where(b == 0, right[:, :128], right[:, 128:]).astype(BF)
        nm[s] = (x * ag_ref[...]).astype(BF)

    for k in (1, 7, 2, 6, 3, 5, 4):
        peer = {"row": lax.rem(zi + k, NZ) * NW + wi}
        send(rg.at[zi, wi], rg.at[zi, wi], 46 + k, peer)
    pass_on(w_part, 6)
    for s in range(2):
        qkv[s, 0] = (mm(nm[s], awt[0]) * (32.0**-0.5)).astype(BF)
        qkv[s, 1] = mm(nm[s], awt[1]).astype(BF)
        qkv[s, 2] = mm(nm[s], awt[2]).astype(BF)
        qkv[s, 3] = jax.nn.sigmoid(mm(nm[s], awt[3])).astype(BF)

    def group(slot, dz):
        return bf.at[slot, pl.ds(lax.rem(zi + NZ - dz, NZ) * NW, NW)]

    for dz in (0, 1, 7, 2, 6, 3, 5, 4):
        arrived(bf.at[0, pl.ds(0, NW if dz else NW - 1)], 13 + dz)
        part = group(q, dz)
        send(part, part, 21 + dz if dz < 4 else 25, right_nb)
        send(part, part, 33 - dz if dz >= 4 else 30, left_nb)
    def relay(n):
        arrived(bf.at[0, pl.ds(0, NW)], 21 + n)
        send(group(q_left, n), group(q_left, n), 31, right_nb)
        arrived(bf.at[0, pl.ds(0, NW)], 26 + n)
        send(group(q_right, 7 - n), group(q_right, 7 - n), 32, left_nb)

    relay(0)
    relay(1)

    w_core = wi + 1 - 2 * (wi % 2)
    w_far = lax.rem(wi + 2, NW)
    other_core = {"row": zi * NW + w_core}
    near, rest = (0, 1, 7, 2, 6), (3, 5, 4)

    def onward(distances, slot, k, where):
        for dz in distances:
            block = rg.at[lax.rem(zi + NZ - dz, NZ), slot]
            send(block, block, k, where)

    def from_z(distances, k):
        for dz in distances:
            if dz:
                arrived(rg.at[0, 0], 46 + dz)
            onward((dz,), wi, k, {"row": zi * NW + w_far})
            onward((dz,), wi, 36, other_core)

    from_z(near, 37)
    relay(2)
    relay(3)
    from_z(rest, 35)

    arrived(lb.at[pl.ds(0, NR - 1)], 33)

    @pl.when(inside)
    def _():
        arrived(rb.at[pl.ds(0, NR // 2 - 1)], 34)

    @pl.when(jnp.logical_not(inside))
    def _():
        arrived(rb, 34)

    tl = lb[...].astype(F32).reshape(256, 256).astype(BF)
    tr = rb[...].astype(F32).reshape(128, 256).astype(BF)
    tb[...] = mm_t(tl, tr).reshape(32, 8, 128).astype(BF)
    bk[r] = tb[r]
    row_peers(lambda peer: send(tb.at[peer], bk.at[r], 39, {"row": peer}))

    lane_head = lax.broadcasted_iota(jnp.int32, (256, 128), 1) // 32
    for s in range(2):
        value = jnp.zeros((256, 128), F32)
        for k in range(NQ):
            h = lax.rem(q + (0, 1, 3, 2)[k], NQ)
            if s == 0 and k == 1:
                arrived(bf.at[0, pl.ds(0, 4 * NW)], 30)
            if s == 0 and k == 2:
                arrived(bf.at[0, pl.ds(0, 4 * NW)], 25)
            if s == 0 and k == 3:
                arrived(bf.at[0, pl.ds(0, 4 * NW)], 31)
                arrived(bf.at[0, pl.ds(0, 4 * NW)], 32)
            here = lane_head == h
            query = jnp.where(here, qkv[s, 0].astype(F32), 0.0).astype(BF)
            score = mm_t(query, qkv[s, 1]) + bf[h].astype(F32).reshape(256, 256)
            expo = jnp.exp(score - jnp.max(score, axis=1, keepdims=True))
            total = jnp.sum(expo, axis=1, keepdims=True)
            value = jnp.where(here, mm(expo.astype(BF), qkv[s, 2]) / total, value)
        mx[b, s] = (qkv[s, 3].astype(F32) * value).astype(BF)
        send(mx.at[b, s], mx.at[b, s], 43 + s, {"branch": 1 - b})

    arrived(rg.at[pl.ds(0, 5), 0], 37)
    onward(near, w_far, 38, other_core)
    arrived(rg.at[pl.ds(0, 3), 0], 35)
    onward(rest, w_far, 38, other_core)

    arrived(rg.at[:, 0], 36)
    arrived(rg.at[:, 0], 38)
    for s in range(2):
        x = rg[:, :, s].astype(F32).reshape(32, 32, 128)
        x = jnp.transpose(x, (1, 0, 2)).astype(BF)
        for d in range(32):
            rgt[32 * s : 32 * s + 32, 128 * d : 128 * d + 128] = x[d]

    for s in range(2):
        arrived(mx.at[0, s], 43 + s)
        x = mm(mx[0, s], mw_ref[0:128]) + mm(mx[1, s], mw_ref[128:256])
        x = mn[:, s, :, cols].astype(F32).reshape(256, 128) + x
        ao[:, s] = x.reshape(32, 8, 128).astype(BF)
        mo[s, r] = ao[r, s]
        row_peers(lambda peer: send(ao.at[peer, s], mo.at[s, r], 45 + s, {"row": peer}))

    arrived(bk.at[pl.ds(0, NR - 1)], 39)
    xs[...] = jnp.transpose(bk[...].astype(F32), (1, 0, 2)).astype(BF)
    xr[q] = xs[pl.ds(2 * q, 2)]
    for k in range(1, NQ):
        peer = lax.rem(q + k, NQ)
        send(xs.at[pl.ds(2 * peer, 2)], xr.at[q], 40, {"seq": peer})

    def outer_step(n, carry):
        x = mm(lxt[...], rgt[:, pl.ds(pl.multiple_of(n * 256, 256), 256)]).astype(BF)
        for d in range(2):
            for i in range(8):
                pq[
                    i // 2,
                    pl.ds(pl.multiple_of(n * 64 + 32 * d, 32), 32),
                    128 * (i % 2) : 128 * (i % 2) + 128,
                ] = x[32 * i : 32 * i + 32, 128 * d : 128 * d + 128]
        return carry

    lax.fori_loop(0, 16, outer_step, 0, unroll=8)

    for n in range(4):
        x = (mm(oot[...], pq[n]) * (1.0 / 256.0)).astype(BF)
        for i in range(2):
            ob[:, 2 * n + i] = x[:, 128 * i : 128 * i + 128].reshape(4, 32, 128)
    orb[q] = ob[q]
    for k in range(1, NQ):
        peer = lax.rem(q + k, NQ)
        send(ob.at[peer], orb.at[q], 42, {"seq": peer})

    for k, c in ((7, 1), (8, 0), (10, 0), (11, 1)):
        arrived(w_part(q, c), k)
    out_w = w[:, 32:64].astype(F32).reshape(128, 128)
    out_w = jnp.transpose(out_w).astype(BF)
    trans_gain = column(cn_ref[...])
    pair_in = jnp.concatenate(
        [g[:, 2 * q + i, :, cols].astype(F32).reshape(128, 128) for i in range(2)], axis=1
    )
    tri_row = jnp.concatenate([tin[2 * q + i, :, cols] for i in range(2)], axis=1)
    gate = jax.nn.sigmoid(mm(w[:, 0:32].reshape(128, 128), tri_row))
    arrived(xr.at[pl.ds(0, NQ - 1)], 40)
    row_tri = jnp.concatenate(
        [xr[:, i].astype(F32).reshape(128, 128) for i in range(2)], axis=1
    )
    first = pair_in + gate * mm(out_w, normalize(row_tri, 0).astype(BF))
    first = first.astype(BF).astype(F32)
    trans = (normalize(first, 0) * trans_gain).astype(BF)
    moved = first
    for k in range(NQ):
        hidden = jnp.maximum(mm(w[k, 64:192], trans), 0.0).astype(BF)
        moved = moved + mm(w[k, 192:320], hidden)
    moved = moved.astype(BF)
    for i in range(2):
        pn[:, i] = moved[:, 128 * i : 128 * i + 128].reshape(4, 32, 128)
    fb[pl.ds(2 * q, 2)] = pn[q]
    for k in range(1, NQ):
        peer = lax.rem(q + k, NQ)
        send(pn.at[peer], fb.at[pl.ds(2 * q, 2)], 41, {"seq": peer})

    arrived(orb.at[pl.ds(0, NQ - 1)], 42)
    update = orb[0].astype(F32)
    for k in range(1, NQ):
        update = update + orb[k].astype(F32)
    update = update.astype(BF).astype(F32)
    arrived(fb.at[pl.ds(0, 6)], 41)
    update = update + fb[...].astype(F32)
    pair_ref[...] = jnp.transpose(update, (1, 0, 2)).reshape(256, 128).astype(BF)

    for s in range(2):
        arrived(mo.at[s, pl.ds(0, NR - 1)], 45 + s)
        msa_ref[256 * s : 256 * s + 256] = mo[s].astype(F32).reshape(256, 128).astype(BF)

    for c in range(2):
        for k in (0, 2, 4):
            left_here(g_part(q, c), k + c)
            left_here(w_part(q, c), 6 + k + c)
    for n in range(8):
        left_here(bf.at[0, pl.ds(0, NW if n else NW - 1)], 13 + n)
    for n in range(1, NZ):
        left_here(rg.at[0, 0], 46 + n)
    for n in range(4):
        left_here(bf.at[0, pl.ds(0, NW)], 21 + n)
        left_here(bf.at[0, pl.ds(0, NW)], 26 + n)
    for k in (25, 30, 31, 32):
        left_here(bf.at[0, pl.ds(0, 4 * NW)], k)
    for k, view in (
        (12, mn.at[pl.ds(0, NR - 1)]),
        (33, lb.at[pl.ds(0, NR - 1)]),
        (35, rg.at[pl.ds(0, 3), 0]),
        (36, rg.at[:, 0]),
        (37, rg.at[pl.ds(0, 5), 0]),
        (38, rg.at[:, 0]),
        (39, bk.at[pl.ds(0, NR - 1)]),
        (40, xr.at[pl.ds(0, NQ - 1)]),
        (41, fb.at[pl.ds(0, 6)]),
        (42, orb.at[pl.ds(0, NQ - 1)]),
        (43, mx.at[0, 0]),
        (44, mx.at[0, 0]),
        (45, mo.at[0, pl.ds(0, NR - 1)]),
        (46, mo.at[0, pl.ds(0, NR - 1)]),
    ):
        left_here(view, k)

    @pl.when(inside)
    def _():
        left_here(lb.at[pl.ds(0, NR - 1)], 34)


def hand_over(msa_in, pair_in, msa_out, pair_out):
    msa_out[...] = msa_in[...]
    pair_out[...] = pair_in[...]


def shards(
    alignment_input,
    pairwise_input,
    alignment_gain,
    product_gain,
    attention_weight,
    mixing_weight,
    outer_input_weight,
    outer_output_weight,
    bias_matrix,
    pairwise_gain,
    triangle_input_weight,
    triangle_gate_weight,
    triangle_gain,
    triangle_output_weight,
    transition_gain,
    transition_up_weight,
    transition_down_weight,
):
    operands = (
        alignment_input.reshape(2, NR, 8, 256),
        pairwise_input,
        alignment_gain.reshape(1, 256),
        product_gain.reshape(1, 256),
        attention_weight,
        mixing_weight,
        outer_input_weight.transpose(1, 2, 0),
        outer_output_weight,
        bias_matrix.T,
        pairwise_gain.reshape(1, 128),
        triangle_input_weight,
        triangle_gate_weight,
        triangle_gain.reshape(1, 32),
        triangle_output_weight.T,
        transition_gain.reshape(1, 128),
        transition_up_weight,
        transition_down_weight,
    )
    vm = pltpu.VMEM
    held = [vm(x.shape, x.dtype) for x in operands]
    held[4] = vm((256, 4, 128), BF)
    held[5] = vm((256, 128), BF)
    msa, pair = pl.pallas_call(
        body,
        out_shape=(
            jax.ShapeDtypeStruct((512, 128), BF),
            jax.ShapeDtypeStruct((256, 128), BF),
        ),
        in_specs=[pl.BlockSpec(memory_space=pltpu.HBM)] * len(operands),
        out_specs=[pl.BlockSpec(memory_space=pltpu.VMEM)] * 2,
        scratch_shapes=held
        + [
            vm((1024, 128), F32),
            vm((4, 256, 128), BF),
            vm((128, 1024), BF),
            vm((4, 8, 32, 256), BF),
            vm((4, 320, 128), BF),
            vm((8, 128, 256), BF),
            vm((8, 32, 256), F32),
            vm((8, 32, 256), F32),
            vm((32, 8, 256), BF),
            vm((32, 8, 256), BF),
            vm((8, 256), BF),
            vm((32, 8, 256), BF),
            vm((16, 8, 256), BF),
            vm((4, 32, 8, 256), BF),
            vm((32, 2, 8, 256), BF),
            vm((2, 256, 256), BF),
            vm((64, 256), F32),
            vm((256, 64), BF),
            vm((2, 4, 256, 128), BF),
            vm((8, 4, 2, 32, 128), BF),
            vm((64, 4096), BF),
            vm((4, 1024, 256), BF),
            vm((4, 8, 32, 128), BF),
            vm((4, 8, 32, 128), BF),
            vm((32, 8, 128), BF),
            vm((32, 8, 128), BF),
            vm((8, 32, 128), BF),
            vm((4, 2, 32, 128), BF),
            vm((4, 2, 32, 128), BF),
            vm((8, 32, 128), BF),
            vm((2, 2, 256, 128), BF),
            vm((32, 2, 8, 128), BF),
            vm((2, 32, 8, 128), BF),
            pltpu.SemaphoreType.DMA((17,)),
            pltpu.SemaphoreType.DMA((54,)),
            pltpu.SemaphoreType.DMA((54,)),
        ],
        compiler_params=pltpu.CompilerParams(
            collective_id=0, has_side_effects=True, vmem_limit_bytes=67_043_328
        ),
    )(*operands)
    msa, pair = pl.pallas_call(
        hand_over,
        out_shape=(
            jax.ShapeDtypeStruct((512, 128), BF),
            jax.ShapeDtypeStruct((256, 128), BF),
        ),
        in_specs=[pl.BlockSpec(memory_space=pltpu.VMEM)] * 2,
        out_specs=[pl.BlockSpec(memory_space=pltpu.VMEM)] * 2,
    )(msa, pair)
    return msa.reshape(64, 8, 128), pair.reshape(32, 8, 128)


def solution(mesh):
    return jax.shard_map(
        shards,
        mesh=mesh,
        in_specs=(
            P("seq", "row", None),
            P("seq", "row", None),
            P(),
            P(),
            P(),
            P(),
            P(),
            P(),
            P(),
            P(),
            P(None, "seq", None),
            P("seq", None),
            P("seq"),
            P(None, "seq"),
            P(),
            P("seq", None),
            P(None, "seq"),
        ),
        out_specs=(P("seq", "row", "branch"), P("seq", "row", "branch")),
        check_vma=False,
    )
```

```python
import jax
import jax.numpy as jnp
from jax import lax
from jax.experimental import pallas as pl
from jax.experimental.pallas import tpu as pltpu
from jax.sharding import PartitionSpec as P

EPSILON = 1e-05
BF = jnp.bfloat16
F32 = jnp.float32
NZ, NW = 8, 4
NR = NZ * NW
NQ = 4


def mm(a, b):
    return jnp.dot(a, b, preferred_element_type=F32)


def mm_t(a, b):
    return lax.dot_general(a, b, (((1,), (1,)), ((), ())), preferred_element_type=F32)


def normalize(x, axis):
    average = jnp.mean(x, axis=axis, keepdims=True)
    centred = x - average
    spread = jnp.mean(centred * centred, axis=axis, keepdims=True)
    return centred * lax.rsqrt(spread + EPSILON)


def column(row):
    n = row.shape[1]
    eye = lax.broadcasted_iota(jnp.int32, (n, n), 0) == lax.broadcasted_iota(
        jnp.int32, (n, n), 1
    )
    return jnp.sum(jnp.where(eye, row, 0.0), axis=1, keepdims=True)


def body(
    a_hbm,
    p_hbm,
    ag_hbm,
    pg_hbm,
    aw_hbm,
    mw_hbm,
    oi_hbm,
    oo_hbm,
    bm_hbm,
    cg_hbm,
    ti_hbm,
    tg_hbm,
    tn_hbm,
    to_hbm,
    cn_hbm,
    up_hbm,
    dn_hbm,
    msa_ref,
    pair_ref,
    a_ref,
    p_ref,
    ag_ref,
    pg_ref,
    aw_ref,
    mw_ref,
    oi_ref,
    oo_ref,
    bm_ref,
    cg_ref,
    ti_ref,
    tg_ref,
    tn_ref,
    to_ref,
    cn_ref,
    up_ref,
    dn_ref,
    awf,
    awt,
    oot,
    g,
    w,
    tin,
    lt,
    rt,
    ls,
    rs,
    bs,
    lb,
    rb,
    bf,
    mn,
    nm,
    lx,
    lxt,
    qkv,
    rg,
    rgt,
    pq,
    ob,
    orb,
    tb,
    bk,
    xs,
    xr,
    pn,
    fb,
    mx,
    ao,
    mo,
    cs,
    ss,
    rv,
):
    b = lax.axis_index("branch")
    r = lax.axis_index("row")
    q = lax.axis_index("seq")
    zi = r // NW
    wi = r % NW
    inside = (r // (NR // 2)) == b
    cols = pl.ds(pl.multiple_of(b * 128, 128), 128)

    loads = {}
    for n, (src, dst) in enumerate(
        (
            (p_hbm, p_ref),
            (a_hbm, a_ref),
            (tg_hbm, tg_ref),
            (tn_hbm, tn_ref),
            (to_hbm, to_ref),
            (up_hbm, up_ref),
            (dn_hbm, dn_ref),
            (pg_hbm, pg_ref),
            (oi_hbm, oi_ref),
            (aw_hbm.at[:, :, cols], aw_ref),
            (oo_hbm, oo_ref),
            (bm_hbm, bm_ref),
            (cg_hbm, cg_ref),
            (ti_hbm, ti_ref),
            (ag_hbm, ag_ref),
            (cn_hbm, cn_ref),
            (mw_hbm.at[:, cols], mw_ref),
        )
    ):
        loads[n] = pltpu.make_async_copy(src, dst, cs.at[n])
        loads[n].start()

    def signal(where):
        pl.semaphore_signal(
            barrier, inc=1, device_id=where, device_id_type=pl.DeviceIdType.MESH
        )

    def send(src, dst, k, where):
        pltpu.make_async_remote_copy(
            src_ref=src,
            dst_ref=dst,
            send_sem=ss.at[k],
            recv_sem=rv.at[k],
            device_id=where,
            device_id_type=pl.DeviceIdType.MESH,
        ).start()

    def arrived(view, k):
        pltpu.make_async_copy(view, view, rv.at[k]).wait()

    def left_here(view, k):
        pltpu.make_async_copy(view, view, ss.at[k]).wait()

    right_nb = {"seq": lax.rem(q + 1, NQ)}
    left_nb = {"seq": lax.rem(q + NQ - 1, NQ)}
    q_right = lax.rem(q + 1, NQ)
    q_left = lax.rem(q + NQ - 1, NQ)

    def both_ways(view, k):
        for c in range(2):
            send(view(q, c), view(q, c), k + c, right_nb)
            send(view(q, c), view(q, c), k + 2 + c, left_nb)

    def pass_on(view, k):
        arrived(view(q, 0), k)
        send(view(q_left, 0), view(q_left, 0), k + 4, right_nb)
        arrived(view(q, 1), k + 3)
        send(view(q_right, 1), view(q_right, 1), k + 5, left_nb)

    def g_part(slot, c):
        return g.at[slot, pl.ds(4 * c, 4)]

    def w_part(slot, c):
        return w.at[slot, pl.ds(160 * c, 160)]

    def row_peers(do):
        for dz in (4, 3, 5, 2, 6, 1, 7, 0):
            for dw in (2, 3, 1, 0):
                if dz or dw:
                    do(lax.rem(zi + dz, NZ) * NW + lax.rem(wi + dw, NW))

    barrier = pltpu.get_barrier_semaphore()
    row_peers(lambda peer: signal({"row": peer}))
    for k in range(1, NQ):
        signal({"seq": lax.rem(q + k, NQ)})
    signal({"branch": 1 - b})

    loads[0].wait()
    g[q] = jnp.transpose(p_ref[...].astype(F32), (1, 0, 2)).astype(BF)
    loads[1].wait()

    pl.semaphore_wait(barrier, NR - 1 + NQ - 1 + 1)

    both_ways(g_part, 0)
    row_peers(lambda peer: send(a_ref.at[:, peer], mn.at[r], 12, {"row": peer}))

    for s in range(2):
        mn[r, s] = a_ref[s, r]
    for n in range(2, 7):
        loads[n].wait()
    w[q, 0:32] = tg_ref[...]
    w[q, 32:64] = (to_ref[...].astype(F32) * column(tn_ref[...])).astype(BF)
    w[q, 64:192] = up_ref[...]
    w[q, 192:320] = dn_ref[...]
    pass_on(g_part, 0)
    loads[7].wait()
    loads[8].wait()
    lane = lax.broadcasted_iota(jnp.int32, (16, 8, 256), 2) // 32
    sub = lax.broadcasted_iota(jnp.int32, (16, 8, 256), 1)
    wide_left = jnp.concatenate([oi_ref[0]] * 8, axis=0)
    for s in range(2):
        for k in range(2):
            x = a_ref[s, 16 * k : 16 * k + 16].astype(F32).reshape(128, 256)
            x = (normalize(x, 1) * pg_ref[...]).astype(BF)
            x = mm_t(x, wide_left).reshape(16, 8, 256)
            lx[32 * s + 16 * k : 32 * s + 16 * k + 16] = jnp.sum(
                jnp.where(lane == sub, x, 0.0), axis=1
            )
    lxt[...] = jnp.transpose(lx[...]).astype(BF)
    loads[9].wait()
    awf[...] = aw_ref[...].astype(F32).reshape(1024, 128)
    for t in range(4):
        awt[t] = awf[pl.ds(t, 256, stride=4)].astype(BF)
    loads[10].wait()
    x = jnp.transpose(oo_ref[...].astype(F32), (1, 0, 2)).reshape(1024, 128)
    oot[...] = jnp.transpose(x).astype(BF)
    for n in range(11, 17):
        loads[n].wait()

    head_row = lax.broadcasted_iota(jnp.int32, (8, 128), 0)
    pick = jnp.where(head_row == NQ * b + q, bm_ref[...].astype(F32), 0.0)
    pick = jnp.sum(pick, axis=0, keepdims=True)
    pair_gain = column(cg_ref[...])

    def bias_row(i, acc):
        unit = normalize(g[:, i].astype(F32).reshape(128, 256), 0)
        tin[i] = (unit * pair_gain).astype(BF)
        return acc + mm(jnp.where(head_row == i, pick, 0.0).astype(BF), unit.astype(BF))

    arrived(g_part(q, 0), 2)
    arrived(g_part(q, 0), 4)
    acc = lax.fori_loop(0, 4, bias_row, jnp.zeros((8, 256), F32), unroll=4)
    arrived(g_part(q, 1), 1)
    arrived(g_part(q, 1), 5)
    bs[...] = lax.fori_loop(4, 8, bias_row, acc, unroll=4).astype(BF)
    bf[q, r] = bs[...]
    for dz in (4, 3, 5, 2, 6, 1, 7, 0):
        for dw in (2, 3, 1, 0):
            if dz or dw:
                peer = lax.rem(zi + dz, NZ) * NW + lax.rem(wi + dw, NW)
                send(bs, bf.at[q, r], 13 + dz, {"row": peer})
    def tri_row_step(i, carry):
        lin = mm(ti_ref[...].reshape(128, 128), tin[i])
        lt[i] = lin[0:32] * jax.nn.sigmoid(lin[32:64])
        rt[i] = lin[64:96] * jax.nn.sigmoid(lin[96:128])
        return carry

    lax.fori_loop(0, 8, tri_row_step, 0, unroll=4)
    ls[...] = jnp.transpose(lt[...], (1, 0, 2)).astype(BF)
    rs[...] = jnp.transpose(rt[...], (1, 0, 2)).astype(BF)
    lb[r] = ls[r]
    row_peers(lambda peer: send(ls.at[peer], lb.at[r], 33, {"row": peer}))

    @pl.when(inside)
    def _():
        rb[r % (NR // 2)] = rs[r]
        row_peers(lambda peer: send(rs.at[peer], rb.at[r % (NR // 2)], 34, {"row": peer}))

    both_ways(w_part, 6)

    arrived(mn.at[pl.ds(0, NR - 1)], 12)
    for s in range(2):
        x = normalize(mn[:, s].astype(F32).reshape(256, 256), 1)
        right = mm_t(oi_ref[1], (x * pg_ref[...]).astype(BF))
        rg[zi, wi, s] = jnp.where(b == 0, right[:, :128], right[:, 128:]).astype(BF)
        nm[s] = (x * ag_ref[...]).astype(BF)

    for k in (1, 7, 2, 6, 3, 5, 4):
        peer = {"row": lax.rem(zi + k, NZ) * NW + wi}
        send(rg.at[zi, wi], rg.at[zi, wi], 46 + k, peer)
    pass_on(w_part, 6)
    for s in range(2):
        qkv[s, 0] = (mm(nm[s], awt[0]) * (32.0**-0.5)).astype(BF)
        qkv[s, 1] = mm(nm[s], awt[1]).astype(BF)
        qkv[s, 2] = mm(nm[s], awt[2]).astype(BF)
        qkv[s, 3] = jax.nn.sigmoid(mm(nm[s], awt[3])).astype(BF)

    def group(slot, dz):
        return bf.at[slot, pl.ds(lax.rem(zi + NZ - dz, NZ) * NW, NW)]

    for dz in (0, 1, 7, 2, 6, 3, 5, 4):
        arrived(bf.at[0, pl.ds(0, NW if dz else NW - 1)], 13 + dz)
        part = group(q, dz)
        send(part, part, 21 + dz if dz < 4 else 25, right_nb)
        send(part, part, 33 - dz if dz >= 4 else 30, left_nb)
    def relay(n):
        arrived(bf.at[0, pl.ds(0, NW)], 21 + n)
        send(group(q_left, n), group(q_left, n), 31, right_nb)
        arrived(bf.at[0, pl.ds(0, NW)], 26 + n)
        send(group(q_right, 7 - n), group(q_right, 7 - n), 32, left_nb)

    relay(0)
    relay(1)

    w_core = wi + 1 - 2 * (wi % 2)
    w_far = lax.rem(wi + 2, NW)
    other_core = {"row": zi * NW + w_core}
    near, rest = (0, 1, 7, 2, 6), (3, 5, 4)

    def onward(distances, slot, k, where):
        for dz in distances:
            block = rg.at[lax.rem(zi + NZ - dz, NZ), slot]
            send(block, block, k, where)

    def from_z(distances, k):
        for dz in distances:
            if dz:
                arrived(rg.at[0, 0], 46 + dz)
            onward((dz,), wi, k, {"row": zi * NW + w_far})
            onward((dz,), wi, 36, other_core)

    from_z(near, 37)
    relay(2)
    relay(3)
    from_z(rest, 35)

    arrived(lb.at[pl.ds(0, NR - 1)], 33)

    @pl.when(inside)
    def _():
        arrived(rb.at[pl.ds(0, NR // 2 - 1)], 34)

    @pl.when(jnp.logical_not(inside))
    def _():
        arrived(rb, 34)

    tl = lb[...].astype(F32).reshape(256, 256).astype(BF)
    tr = rb[...].astype(F32).reshape(128, 256).astype(BF)
    tb[...] = mm_t(tl, tr).reshape(32, 8, 128).astype(BF)
    bk[r] = tb[r]
    row_peers(lambda peer: send(tb.at[peer], bk.at[r], 39, {"row": peer}))

    lane_head = lax.broadcasted_iota(jnp.int32, (256, 128), 1) // 32
    for s in range(2):
        value = jnp.zeros((256, 128), F32)
        for k in range(NQ):
            h = lax.rem(q + (0, 1, 3, 2)[k], NQ)
            if s == 0 and k == 1:
                arrived(bf.at[0, pl.ds(0, 4 * NW)], 30)
            if s == 0 and k == 2:
                arrived(bf.at[0, pl.ds(0, 4 * NW)], 25)
            if s == 0 and k == 3:
                arrived(bf.at[0, pl.ds(0, 4 * NW)], 31)
                arrived(bf.at[0, pl.ds(0, 4 * NW)], 32)
            here = lane_head == h
            query = jnp.where(here, qkv[s, 0].astype(F32), 0.0).astype(BF)
            score = mm_t(query, qkv[s, 1]) + bf[h].astype(F32).reshape(256, 256)
            expo = jnp.exp(score - jnp.max(score, axis=1, keepdims=True))
            total = jnp.sum(expo, axis=1, keepdims=True)
            value = jnp.where(here, mm(expo.astype(BF), qkv[s, 2]) / total, value)
        mx[b, s] = (qkv[s, 3].astype(F32) * value).astype(BF)
        send(mx.at[b, s], mx.at[b, s], 43 + s, {"branch": 1 - b})

    arrived(rg.at[pl.ds(0, 5), 0], 37)
    onward(near, w_far, 38, other_core)
    arrived(rg.at[pl.ds(0, 3), 0], 35)
    onward(rest, w_far, 38, other_core)

    arrived(rg.at[:, 0], 36)
    arrived(rg.at[:, 0], 38)
    for s in range(2):
        x = rg[:, :, s].astype(F32).reshape(32, 32, 128)
        x = jnp.transpose(x, (1, 0, 2)).astype(BF)
        for d in range(32):
            rgt[32 * s : 32 * s + 32, 128 * d : 128 * d + 128] = x[d]

    for s in range(2):
        arrived(mx.at[0, s], 43 + s)
        x = mm(mx[0, s], mw_ref[0:128]) + mm(mx[1, s], mw_ref[128:256])
        x = mn[:, s, :, cols].astype(F32).reshape(256, 128) + x
        ao[:, s] = x.reshape(32, 8, 128).astype(BF)
        mo[s, r] = ao[r, s]
        row_peers(lambda peer: send(ao.at[peer, s], mo.at[s, r], 45 + s, {"row": peer}))

    arrived(bk.at[pl.ds(0, NR - 1)], 39)
    xs[...] = jnp.transpose(bk[...].astype(F32), (1, 0, 2)).astype(BF)
    xr[q] = xs[pl.ds(2 * q, 2)]
    for k in (2, 1, 3):
        peer = lax.rem(q + k, NQ)
        send(xs.at[pl.ds(2 * peer, 2)], xr.at[q], 40, {"seq": peer})

    def outer_step(n, carry):
        x = mm(lxt[...], rgt[:, pl.ds(pl.multiple_of(n * 256, 256), 256)]).astype(BF)
        for d in range(2):
            for i in range(8):
                pq[
                    i // 2,
                    pl.ds(pl.multiple_of(n * 64 + 32 * d, 32), 32),
                    128 * (i % 2) : 128 * (i % 2) + 128,
                ] = x[32 * i : 32 * i + 32, 128 * d : 128 * d + 128]
        return carry

    lax.fori_loop(0, 16, outer_step, 0, unroll=8)

    for n in range(4):
        x = (mm(oot[...], pq[n]) * (1.0 / 256.0)).astype(BF)
        for i in range(2):
            ob[:, 2 * n + i] = x[:, 128 * i : 128 * i + 128].reshape(4, 32, 128)
    orb[q] = ob[q]
    for k in (2, 1, 3):
        peer = lax.rem(q + k, NQ)
        send(ob.at[peer], orb.at[q], 42, {"seq": peer})

    for k, c in ((7, 1), (8, 0), (10, 0), (11, 1)):
        arrived(w_part(q, c), k)
    out_w = w[:, 32:64].astype(F32).reshape(128, 128)
    out_w = jnp.transpose(out_w).astype(BF)
    trans_gain = column(cn_ref[...])
    pair_in = jnp.concatenate(
        [g[:, 2 * q + i, :, cols].astype(F32).reshape(128, 128) for i in range(2)], axis=1
    )
    tri_row = jnp.concatenate([tin[2 * q + i, :, cols] for i in range(2)], axis=1)
    gate = jax.nn.sigmoid(mm(w[:, 0:32].reshape(128, 128), tri_row))
    arrived(xr.at[pl.ds(0, NQ - 1)], 40)
    row_tri = jnp.concatenate(
        [xr[:, i].astype(F32).reshape(128, 128) for i in range(2)], axis=1
    )
    first = pair_in + gate * mm(out_w, normalize(row_tri, 0).astype(BF))
    first = first.astype(BF).astype(F32)
    trans = (normalize(first, 0) * trans_gain).astype(BF)
    moved = first
    for k in range(NQ):
        hidden = jnp.maximum(mm(w[k, 64:192], trans), 0.0).astype(BF)
        moved = moved + mm(w[k, 192:320], hidden)
    moved = moved.astype(BF)
    for i in range(2):
        pn[:, i] = moved[:, 128 * i : 128 * i + 128].reshape(4, 32, 128)
    fb[pl.ds(2 * q, 2)] = pn[q]
    for k in (2, 1, 3):
        peer = lax.rem(q + k, NQ)
        send(pn.at[peer], fb.at[pl.ds(2 * q, 2)], 41, {"seq": peer})

    arrived(orb.at[pl.ds(0, NQ - 1)], 42)
    update = orb[0].astype(F32)
    for k in range(1, NQ):
        update = update + orb[k].astype(F32)
    update = update.astype(BF).astype(F32)
    arrived(fb.at[pl.ds(0, 6)], 41)
    update = update + fb[...].astype(F32)
    pair_ref[...] = jnp.transpose(update, (1, 0, 2)).reshape(256, 128).astype(BF)

    for s in range(2):
        arrived(mo.at[s, pl.ds(0, NR - 1)], 45 + s)
        msa_ref[256 * s : 256 * s + 256] = mo[s].astype(F32).reshape(256, 128).astype(BF)

    for c in range(2):
        for k in (0, 2, 4):
            left_here(g_part(q, c), k + c)
            left_here(w_part(q, c), 6 + k + c)
    for n in range(8):
        left_here(bf.at[0, pl.ds(0, NW if n else NW - 1)], 13 + n)
    for n in range(1, NZ):
        left_here(rg.at[0, 0], 46 + n)
    for n in range(4):
        left_here(bf.at[0, pl.ds(0, NW)], 21 + n)
        left_here(bf.at[0, pl.ds(0, NW)], 26 + n)
    for k in (25, 30, 31, 32):
        left_here(bf.at[0, pl.ds(0, 4 * NW)], k)
    for k, view in (
        (12, mn.at[pl.ds(0, NR - 1)]),
        (33, lb.at[pl.ds(0, NR - 1)]),
        (35, rg.at[pl.ds(0, 3), 0]),
        (36, rg.at[:, 0]),
        (37, rg.at[pl.ds(0, 5), 0]),
        (38, rg.at[:, 0]),
        (39, bk.at[pl.ds(0, NR - 1)]),
        (40, xr.at[pl.ds(0, NQ - 1)]),
        (41, fb.at[pl.ds(0, 6)]),
        (42, orb.at[pl.ds(0, NQ - 1)]),
        (43, mx.at[0, 0]),
        (44, mx.at[0, 0]),
        (45, mo.at[0, pl.ds(0, NR - 1)]),
        (46, mo.at[0, pl.ds(0, NR - 1)]),
    ):
        left_here(view, k)

    @pl.when(inside)
    def _():
        left_here(lb.at[pl.ds(0, NR - 1)], 34)


def hand_over(msa_in, pair_in, msa_out, pair_out, sems):
    copies = (
        pltpu.make_async_copy(msa_in, msa_out, sems.at[0]),
        pltpu.make_async_copy(pair_in, pair_out, sems.at[1]),
    )
    for copy in copies:
        copy.start()
    for copy in copies:
        copy.wait()


def shards(
    alignment_input,
    pairwise_input,
    alignment_gain,
    product_gain,
    attention_weight,
    mixing_weight,
    outer_input_weight,
    outer_output_weight,
    bias_matrix,
    pairwise_gain,
    triangle_input_weight,
    triangle_gate_weight,
    triangle_gain,
    triangle_output_weight,
    transition_gain,
    transition_up_weight,
    transition_down_weight,
):
    operands = (
        alignment_input.reshape(2, NR, 8, 256),
        pairwise_input,
        alignment_gain.reshape(1, 256),
        product_gain.reshape(1, 256),
        attention_weight,
        mixing_weight,
        outer_input_weight.transpose(1, 2, 0),
        outer_output_weight,
        bias_matrix.T,
        pairwise_gain.reshape(1, 128),
        triangle_input_weight,
        triangle_gate_weight,
        triangle_gain.reshape(1, 32),
        triangle_output_weight.T,
        transition_gain.reshape(1, 128),
        transition_up_weight,
        transition_down_weight,
    )
    vm = pltpu.VMEM
    held = [vm(x.shape, x.dtype) for x in operands]
    held[4] = vm((256, 4, 128), BF)
    held[5] = vm((256, 128), BF)
    msa, pair = pl.pallas_call(
        body,
        out_shape=(pltpu.VMEM((512, 128), BF), pltpu.VMEM((256, 128), BF)),
        in_specs=[pl.BlockSpec(memory_space=pltpu.HBM)] * len(operands),
        out_specs=[pl.BlockSpec(memory_space=pltpu.VMEM)] * 2,
        scratch_shapes=held
        + [
            vm((1024, 128), F32),
            vm((4, 256, 128), BF),
            vm((128, 1024), BF),
            vm((4, 8, 32, 256), BF),
            vm((4, 320, 128), BF),
            vm((8, 128, 256), BF),
            vm((8, 32, 256), F32),
            vm((8, 32, 256), F32),
            vm((32, 8, 256), BF),
            vm((32, 8, 256), BF),
            vm((8, 256), BF),
            vm((32, 8, 256), BF),
            vm((16, 8, 256), BF),
            vm((4, 32, 8, 256), BF),
            vm((32, 2, 8, 256), BF),
            vm((2, 256, 256), BF),
            vm((64, 256), F32),
            vm((256, 64), BF),
            vm((2, 4, 256, 128), BF),
            vm((8, 4, 2, 32, 128), BF),
            vm((64, 4096), BF),
            vm((4, 1024, 256), BF),
            vm((4, 8, 32, 128), BF),
            vm((4, 8, 32, 128), BF),
            vm((32, 8, 128), BF),
            vm((32, 8, 128), BF),
            vm((8, 32, 128), BF),
            vm((4, 2, 32, 128), BF),
            vm((4, 2, 32, 128), BF),
            vm((8, 32, 128), BF),
            vm((2, 2, 256, 128), BF),
            vm((32, 2, 8, 128), BF),
            vm((2, 32, 8, 128), BF),
            pltpu.SemaphoreType.DMA((17,)),
            pltpu.SemaphoreType.DMA((54,)),
            pltpu.SemaphoreType.DMA((54,)),
        ],
        compiler_params=pltpu.CompilerParams(
            collective_id=0, has_side_effects=True, vmem_limit_bytes=48 * 2**20
        ),
    )(*(pltpu.with_memory_space_constraint(x, pltpu.HBM) for x in operands))
    msa, pair = pl.pallas_call(
        hand_over,
        out_shape=(
            jax.ShapeDtypeStruct((512, 128), BF),
            jax.ShapeDtypeStruct((256, 128), BF),
        ),
        in_specs=[pl.BlockSpec(memory_space=pltpu.VMEM)] * 2,
        out_specs=[pl.BlockSpec(memory_space=pltpu.HBM)] * 2,
        scratch_shapes=[pltpu.SemaphoreType.DMA((2,))],
    )(*(pltpu.with_memory_space_constraint(x, pltpu.VMEM) for x in (msa, pair)))
    return msa.reshape(64, 8, 128), pair.reshape(32, 8, 128)


def solution(mesh):
    return jax.shard_map(
        shards,
        mesh=mesh,
        in_specs=(
            P("seq", "row", None),
            P("seq", "row", None),
            P(),
            P(),
            P(),
            P(),
            P(),
            P(),
            P(),
            P(),
            P(None, "seq", None),
            P("seq", None),
            P("seq"),
            P(None, "seq"),
            P(),
            P("seq", None),
            P(None, "seq"),
        ),
        out_specs=(P("seq", "row", "branch"), P("seq", "row", "branch")),
        check_vma=False,
    )
```

```python
import jax
import jax.numpy as jnp
from jax import lax
from jax.experimental import pallas as pl
from jax.experimental.pallas import tpu as pltpu
from jax.sharding import PartitionSpec as P

EPSILON = 1e-05
BF = jnp.bfloat16
F32 = jnp.float32
NZ, NW = 8, 4
NR = NZ * NW
NQ = 4


def mm(a, b):
    return jnp.dot(a, b, preferred_element_type=F32)


def mm_t(a, b):
    return lax.dot_general(a, b, (((1,), (1,)), ((), ())), preferred_element_type=F32)


def normalize(x, axis):
    average = jnp.mean(x, axis=axis, keepdims=True)
    centred = x - average
    spread = jnp.mean(centred * centred, axis=axis, keepdims=True)
    return centred * lax.rsqrt(spread + EPSILON)


def column(row):
    n = row.shape[1]
    eye = lax.broadcasted_iota(jnp.int32, (n, n), 0) == lax.broadcasted_iota(
        jnp.int32, (n, n), 1
    )
    return jnp.sum(jnp.where(eye, row, 0.0), axis=1, keepdims=True)


def body(
    a_hbm,
    p_hbm,
    ag_hbm,
    pg_hbm,
    aw_hbm,
    mw_hbm,
    oi_hbm,
    oo_hbm,
    bm_hbm,
    cg_hbm,
    ti_hbm,
    tg_hbm,
    tn_hbm,
    to_hbm,
    cn_hbm,
    up_hbm,
    dn_hbm,
    msa_ref,
    pair_ref,
    a_ref,
    p_ref,
    ag_ref,
    pg_ref,
    aw_ref,
    mw_ref,
    oi_ref,
    oo_ref,
    bm_ref,
    cg_ref,
    ti_ref,
    tg_ref,
    tn_ref,
    to_ref,
    cn_ref,
    up_ref,
    dn_ref,
    awf,
    awt,
    oot,
    g,
    w,
    tin,
    lt,
    rt,
    ls,
    rs,
    bs,
    lb,
    rb,
    bf,
    mn,
    nm,
    lx,
    lxt,
    qkv,
    rg,
    rgt,
    pq,
    ob,
    orb,
    tb,
    bk,
    xs,
    xr,
    pn,
    fb,
    mx,
    ao,
    mo,
    cs,
    ss,
    rv,
):
    b = lax.axis_index("branch")
    r = lax.axis_index("row")
    q = lax.axis_index("seq")
    zi = r // NW
    wi = r % NW
    inside = (r // (NR // 2)) == b
    cols = pl.ds(pl.multiple_of(b * 128, 128), 128)

    def signal(where):
        pl.semaphore_signal(
            barrier, inc=1, device_id=where, device_id_type=pl.DeviceIdType.MESH
        )

    def send(src, dst, k, where):
        pltpu.make_async_remote_copy(
            src_ref=src,
            dst_ref=dst,
            send_sem=ss.at[k],
            recv_sem=rv.at[k],
            device_id=where,
            device_id_type=pl.DeviceIdType.MESH,
        ).start()

    def arrived(view, k):
        pltpu.make_async_copy(view, view, rv.at[k]).wait()

    def left_here(view, k):
        pltpu.make_async_copy(view, view, ss.at[k]).wait()

    right_nb = {"seq": lax.rem(q + 1, NQ)}
    left_nb = {"seq": lax.rem(q + NQ - 1, NQ)}
    q_right = lax.rem(q + 1, NQ)
    q_left = lax.rem(q + NQ - 1, NQ)

    def both_ways(view, k):
        for c in range(2):
            send(view(q, c), view(q, c), k + c, right_nb)
            send(view(q, c), view(q, c), k + 2 + c, left_nb)

    def pass_on(view, k):
        arrived(view(q, 0), k)
        send(view(q_left, 0), view(q_left, 0), k + 4, right_nb)
        arrived(view(q, 1), k + 3)
        send(view(q_right, 1), view(q_right, 1), k + 5, left_nb)

    def g_part(slot, c):
        return g.at[slot, pl.ds(4 * c, 4)]

    def w_part(slot, c):
        return w.at[slot, pl.ds(160 * c, 160)]

    def row_peers(do):
        for dz in (4, 3, 5, 2, 6, 1, 7, 0):
            for dw in (2, 3, 1, 0):
                if dz or dw:
                    do(lax.rem(zi + dz, NZ) * NW + lax.rem(wi + dw, NW))

    loads = {}
    for n, (src, dst) in enumerate(
        (
            (p_hbm, p_ref),
            (a_hbm, a_ref),
            (tg_hbm, tg_ref),
            (tn_hbm, tn_ref),
            (to_hbm, to_ref),
            (up_hbm, up_ref),
            (dn_hbm, dn_ref),
            (pg_hbm, pg_ref),
            (oi_hbm, oi_ref),
            (aw_hbm.at[:, :, cols], aw_ref),
            (oo_hbm, oo_ref),
            (bm_hbm, bm_ref),
            (cg_hbm, cg_ref),
            (ti_hbm, ti_ref),
            (ag_hbm, ag_ref),
            (cn_hbm, cn_ref),
            (mw_hbm.at[:, cols], mw_ref),
        )
    ):
        loads[n] = pltpu.make_async_copy(src, dst, cs.at[n])
    loads[0].start()
    barrier = pltpu.get_barrier_semaphore()
    row_peers(lambda peer: signal({"row": peer}))
    for k in range(1, NQ):
        signal({"seq": lax.rem(q + k, NQ)})
    signal({"branch": 1 - b})
    for n in range(1, len(loads)):
        loads[n].start()

    loads[0].wait()
    g[q] = jnp.transpose(p_ref[...].astype(F32), (1, 0, 2)).astype(BF)
    loads[1].wait()

    pl.semaphore_wait(barrier, NR - 1 + NQ - 1 + 1)

    both_ways(g_part, 0)
    row_peers(lambda peer: send(a_ref.at[:, peer], mn.at[r], 12, {"row": peer}))

    for s in range(2):
        mn[r, s] = a_ref[s, r]
    for n in range(2, 7):
        loads[n].wait()
    w[q, 0:32] = tg_ref[...]
    w[q, 32:64] = (to_ref[...].astype(F32) * column(tn_ref[...])).astype(BF)
    w[q, 64:192] = up_ref[...]
    w[q, 192:320] = dn_ref[...]
    pass_on(g_part, 0)
    loads[7].wait()
    loads[8].wait()
    lane = lax.broadcasted_iota(jnp.int32, (16, 8, 256), 2) // 32
    sub = lax.broadcasted_iota(jnp.int32, (16, 8, 256), 1)
    wide_left = jnp.concatenate([oi_ref[0]] * 8, axis=0)
    for s in range(2):
        for k in range(2):
            x = a_ref[s, 16 * k : 16 * k + 16].astype(F32).reshape(128, 256)
            x = (normalize(x, 1) * pg_ref[...]).astype(BF)
            x = mm_t(x, wide_left).reshape(16, 8, 256)
            lx[32 * s + 16 * k : 32 * s + 16 * k + 16] = jnp.sum(
                jnp.where(lane == sub, x, 0.0), axis=1
            )
    lxt[...] = jnp.transpose(lx[...]).astype(BF)
    loads[9].wait()
    awf[...] = aw_ref[...].astype(F32).reshape(1024, 128)
    for t in range(4):
        awt[t] = awf[pl.ds(t, 256, stride=4)].astype(BF)
    loads[10].wait()
    x = jnp.transpose(oo_ref[...].astype(F32), (1, 0, 2)).reshape(1024, 128)
    oot[...] = jnp.transpose(x).astype(BF)
    for n in range(11, 17):
        loads[n].wait()

    head_row = lax.broadcasted_iota(jnp.int32, (8, 128), 0)
    pick = jnp.where(head_row == NQ * b + q, bm_ref[...].astype(F32), 0.0)
    pick = jnp.sum(pick, axis=0, keepdims=True)
    pair_gain = column(cg_ref[...])

    def bias_row(i, acc):
        unit = normalize(g[:, i].astype(F32).reshape(128, 256), 0)
        tin[i] = (unit * pair_gain).astype(BF)
        return acc + mm(jnp.where(head_row == i, pick, 0.0).astype(BF), unit.astype(BF))

    arrived(g_part(q, 0), 2)
    arrived(g_part(q, 0), 4)
    acc = lax.fori_loop(0, 4, bias_row, jnp.zeros((8, 256), F32), unroll=4)
    arrived(g_part(q, 1), 1)
    arrived(g_part(q, 1), 5)
    bs[...] = lax.fori_loop(4, 8, bias_row, acc, unroll=4).astype(BF)
    bf[q, r] = bs[...]
    for dz in (4, 3, 5, 2, 6, 1, 7, 0):
        for dw in (2, 3, 1, 0):
            if dz or dw:
                peer = lax.rem(zi + dz, NZ) * NW + lax.rem(wi + dw, NW)
                send(bs, bf.at[q, r], 13 + dz, {"row": peer})
    def tri_row_step(i, carry):
        lin = mm(ti_ref[...].reshape(128, 128), tin[i])
        lt[i] = lin[0:32] * jax.nn.sigmoid(lin[32:64])
        rt[i] = lin[64:96] * jax.nn.sigmoid(lin[96:128])
        return carry

    lax.fori_loop(0, 8, tri_row_step, 0, unroll=4)
    ls[...] = jnp.transpose(lt[...], (1, 0, 2)).astype(BF)
    rs[...] = jnp.transpose(rt[...], (1, 0, 2)).astype(BF)
    lb[r] = ls[r]
    row_peers(lambda peer: send(ls.at[peer], lb.at[r], 33, {"row": peer}))

    @pl.when(inside)
    def _():
        rb[r % (NR // 2)] = rs[r]
        row_peers(lambda peer: send(rs.at[peer], rb.at[r % (NR // 2)], 34, {"row": peer}))

    both_ways(w_part, 6)

    arrived(mn.at[pl.ds(0, NR - 1)], 12)
    for s in range(2):
        x = normalize(mn[:, s].astype(F32).reshape(256, 256), 1)
        right = mm_t(oi_ref[1], (x * pg_ref[...]).astype(BF))
        rg[zi, wi, s] = jnp.where(b == 0, right[:, :128], right[:, 128:]).astype(BF)
        nm[s] = (x * ag_ref[...]).astype(BF)

    for k in (1, 7, 2, 6, 3, 5, 4):
        peer = {"row": lax.rem(zi + k, NZ) * NW + wi}
        send(rg.at[zi, wi], rg.at[zi, wi], 46 + k, peer)
    pass_on(w_part, 6)
    for s in range(2):
        qkv[s, 0] = (mm(nm[s], awt[0]) * (32.0**-0.5)).astype(BF)
        qkv[s, 1] = mm(nm[s], awt[1]).astype(BF)
        qkv[s, 2] = mm(nm[s], awt[2]).astype(BF)
        qkv[s, 3] = jax.nn.sigmoid(mm(nm[s], awt[3])).astype(BF)

    def group(slot, dz):
        return bf.at[slot, pl.ds(lax.rem(zi + NZ - dz, NZ) * NW, NW)]

    for dz in (0, 1, 7, 2, 6, 3, 5, 4):
        arrived(bf.at[0, pl.ds(0, NW if dz else NW - 1)], 13 + dz)
        part = group(q, dz)
        send(part, part, 31 if dz < 4 else 32, {"seq": lax.rem(q + 2, NQ)})
        send(part, part, 21 + dz if dz < 4 else 25, right_nb)
        send(part, part, 33 - dz if dz >= 4 else 30, left_nb)
    w_core = wi + 1 - 2 * (wi % 2)
    w_far = lax.rem(wi + 2, NW)
    other_core = {"row": zi * NW + w_core}
    near, rest = (0, 1, 7, 2, 6), (3, 5, 4)

    def onward(distances, slot, k, where):
        for dz in distances:
            block = rg.at[lax.rem(zi + NZ - dz, NZ), slot]
            send(block, block, k, where)

    def from_z(distances, k):
        for dz in distances:
            if dz:
                arrived(rg.at[0, 0], 46 + dz)
            onward((dz,), wi, k, {"row": zi * NW + w_far})
            onward((dz,), wi, 36, other_core)

    from_z(near, 37)
    from_z(rest, 35)

    arrived(lb.at[pl.ds(0, NR - 1)], 33)

    @pl.when(inside)
    def _():
        arrived(rb.at[pl.ds(0, NR // 2 - 1)], 34)

    @pl.when(jnp.logical_not(inside))
    def _():
        arrived(rb, 34)

    tl = lb[...].astype(F32).reshape(256, 256).astype(BF)
    tr = rb[...].astype(F32).reshape(128, 256).astype(BF)
    tb[...] = mm_t(tl, tr).reshape(32, 8, 128).astype(BF)
    bk[r] = tb[r]
    row_peers(lambda peer: send(tb.at[peer], bk.at[r], 39, {"row": peer}))

    lane_head = lax.broadcasted_iota(jnp.int32, (256, 128), 1) // 32
    for s in range(2):
        value = jnp.zeros((256, 128), F32)
        for k in range(NQ):
            h = lax.rem(q + (0, 1, 3, 2)[k], NQ)
            if s == 0 and k == 1:
                arrived(bf.at[0, pl.ds(0, 4 * NW)], 30)
                for n in range(4):
                    arrived(bf.at[0, pl.ds(0, NW)], 26 + n)
            if s == 0 and k == 2:
                arrived(bf.at[0, pl.ds(0, 4 * NW)], 25)
                for n in range(4):
                    arrived(bf.at[0, pl.ds(0, NW)], 21 + n)
            if s == 0 and k == 3:
                arrived(bf.at[0, pl.ds(0, 4 * NW)], 31)
                arrived(bf.at[0, pl.ds(0, 4 * NW)], 32)
            here = lane_head == h
            query = jnp.where(here, qkv[s, 0].astype(F32), 0.0).astype(BF)
            score = mm_t(query, qkv[s, 1]) + bf[h].astype(F32).reshape(256, 256)
            expo = jnp.exp(score - jnp.max(score, axis=1, keepdims=True))
            total = jnp.sum(expo, axis=1, keepdims=True)
            value = jnp.where(here, mm(expo.astype(BF), qkv[s, 2]) / total, value)
        mx[b, s] = (qkv[s, 3].astype(F32) * value).astype(BF)
        send(mx.at[b, s], mx.at[b, s], 43 + s, {"branch": 1 - b})

    arrived(rg.at[pl.ds(0, 5), 0], 37)
    onward(near, w_far, 38, other_core)
    arrived(rg.at[pl.ds(0, 3), 0], 35)
    onward(rest, w_far, 38, other_core)

    arrived(rg.at[:, 0], 36)
    arrived(rg.at[:, 0], 38)
    for s in range(2):
        x = rg[:, :, s].astype(F32).reshape(32, 32, 128)
        x = jnp.transpose(x, (1, 0, 2)).astype(BF)
        for d in range(32):
            rgt[32 * s : 32 * s + 32, 128 * d : 128 * d + 128] = x[d]

    for s in range(2):
        arrived(mx.at[0, s], 43 + s)
        x = mm(mx[0, s], mw_ref[0:128]) + mm(mx[1, s], mw_ref[128:256])
        x = mn[:, s, :, cols].astype(F32).reshape(256, 128) + x
        ao[:, s] = x.reshape(32, 8, 128).astype(BF)
        mo[s, r] = ao[r, s]
        row_peers(lambda peer: send(ao.at[peer, s], mo.at[s, r], 45 + s, {"row": peer}))

    arrived(bk.at[pl.ds(0, NR - 1)], 39)
    xs[...] = jnp.transpose(bk[...].astype(F32), (1, 0, 2)).astype(BF)
    xr[q] = xs[pl.ds(2 * q, 2)]
    for k in (2, 1, 3):
        peer = lax.rem(q + k, NQ)
        send(xs.at[pl.ds(2 * peer, 2)], xr.at[q], 40, {"seq": peer})

    def outer_step(n, carry):
        x = mm(lxt[...], rgt[:, pl.ds(pl.multiple_of(n * 256, 256), 256)]).astype(BF)
        for d in range(2):
            for i in range(8):
                pq[
                    i // 2,
                    pl.ds(pl.multiple_of(n * 64 + 32 * d, 32), 32),
                    128 * (i % 2) : 128 * (i % 2) + 128,
                ] = x[32 * i : 32 * i + 32, 128 * d : 128 * d + 128]
        return carry

    lax.fori_loop(0, 16, outer_step, 0, unroll=8)

    for n in range(4):
        x = (mm(oot[...], pq[n]) * (1.0 / 256.0)).astype(BF)
        for i in range(2):
            ob[:, 2 * n + i] = x[:, 128 * i : 128 * i + 128].reshape(4, 32, 128)
    orb[q] = ob[q]
    for k in (2, 1, 3):
        peer = lax.rem(q + k, NQ)
        send(ob.at[peer], orb.at[q], 42, {"seq": peer})

    for k, c in ((7, 1), (8, 0), (10, 0), (11, 1)):
        arrived(w_part(q, c), k)
    out_w = w[:, 32:64].astype(F32).reshape(128, 128)
    out_w = jnp.transpose(out_w).astype(BF)
    trans_gain = column(cn_ref[...])
    pair_in = jnp.concatenate(
        [g[:, 2 * q + i, :, cols].astype(F32).reshape(128, 128) for i in range(2)], axis=1
    )
    tri_row = jnp.concatenate([tin[2 * q + i, :, cols] for i in range(2)], axis=1)
    gate = jax.nn.sigmoid(mm(w[:, 0:32].reshape(128, 128), tri_row))
    arrived(xr.at[pl.ds(0, NQ - 1)], 40)
    row_tri = jnp.concatenate(
        [xr[:, i].astype(F32).reshape(128, 128) for i in range(2)], axis=1
    )
    first = pair_in + gate * mm(out_w, normalize(row_tri, 0).astype(BF))
    first = first.astype(BF).astype(F32)
    trans = (normalize(first, 0) * trans_gain).astype(BF)
    moved = first
    for k in range(NQ):
        hidden = jnp.maximum(mm(w[k, 64:192], trans), 0.0).astype(BF)
        moved = moved + mm(w[k, 192:320], hidden)
    moved = moved.astype(BF)
    for i in range(2):
        pn[:, i] = moved[:, 128 * i : 128 * i + 128].reshape(4, 32, 128)
    fb[pl.ds(2 * q, 2)] = pn[q]
    for k in (2, 1, 3):
        peer = lax.rem(q + k, NQ)
        send(pn.at[peer], fb.at[pl.ds(2 * q, 2)], 41, {"seq": peer})

    for c in range(2):
        for k in (0, 2, 4):
            left_here(g_part(q, c), k + c)
            left_here(w_part(q, c), 6 + k + c)
    for n in range(8):
        left_here(bf.at[0, pl.ds(0, NW if n else NW - 1)], 13 + n)
    for n in range(1, NZ):
        left_here(rg.at[0, 0], 46 + n)
    for n in range(4):
        left_here(bf.at[0, pl.ds(0, NW)], 21 + n)
        left_here(bf.at[0, pl.ds(0, NW)], 26 + n)
    for k in (25, 30, 31, 32):
        left_here(bf.at[0, pl.ds(0, 4 * NW)], k)
    for k, view in (
        (12, mn.at[pl.ds(0, NR - 1)]),
        (33, lb.at[pl.ds(0, NR - 1)]),
        (35, rg.at[pl.ds(0, 3), 0]),
        (36, rg.at[:, 0]),
        (37, rg.at[pl.ds(0, 5), 0]),
        (38, rg.at[:, 0]),
        (39, bk.at[pl.ds(0, NR - 1)]),
        (40, xr.at[pl.ds(0, NQ - 1)]),
        (43, mx.at[0, 0]),
        (44, mx.at[0, 0]),
    ):
        left_here(view, k)

    @pl.when(inside)
    def _():
        left_here(lb.at[pl.ds(0, NR - 1)], 34)

    arrived(orb.at[pl.ds(0, NQ - 1)], 42)
    update = orb[0].astype(F32)
    for k in range(1, NQ):
        update = update + orb[k].astype(F32)
    update = update.astype(BF).astype(F32)
    arrived(fb.at[pl.ds(0, 6)], 41)
    update = update + fb[...].astype(F32)
    pair_ref[...] = jnp.transpose(update, (1, 0, 2)).reshape(256, 128).astype(BF)

    for s in range(2):
        arrived(mo.at[s, pl.ds(0, NR - 1)], 45 + s)
        msa_ref[256 * s : 256 * s + 256] = mo[s].astype(F32).reshape(256, 128).astype(BF)

    left_here(fb.at[pl.ds(0, 6)], 41)
    left_here(orb.at[pl.ds(0, NQ - 1)], 42)
    for s in range(2):
        left_here(mo.at[0, pl.ds(0, NR - 1)], 45 + s)


def hand_over(msa_in, pair_in, msa_out, pair_out, sems):
    copies = (
        pltpu.make_async_copy(msa_in, msa_out, sems.at[0]),
        pltpu.make_async_copy(pair_in, pair_out, sems.at[1]),
    )
    for copy in copies:
        copy.start()
    for copy in copies:
        copy.wait()


def shards(
    alignment_input,
    pairwise_input,
    alignment_gain,
    product_gain,
    attention_weight,
    mixing_weight,
    outer_input_weight,
    outer_output_weight,
    bias_matrix,
    pairwise_gain,
    triangle_input_weight,
    triangle_gate_weight,
    triangle_gain,
    triangle_output_weight,
    transition_gain,
    transition_up_weight,
    transition_down_weight,
):
    operands = (
        alignment_input.reshape(2, NR, 8, 256),
        pairwise_input,
        alignment_gain.reshape(1, 256),
        product_gain.reshape(1, 256),
        attention_weight,
        mixing_weight,
        outer_input_weight.transpose(1, 2, 0),
        outer_output_weight,
        bias_matrix.T,
        pairwise_gain.reshape(1, 128),
        triangle_input_weight,
        triangle_gate_weight,
        triangle_gain.reshape(1, 32),
        triangle_output_weight.T,
        transition_gain.reshape(1, 128),
        transition_up_weight,
        transition_down_weight,
    )
    vm = pltpu.VMEM
    held = [vm(x.shape, x.dtype) for x in operands]
    held[4] = vm((256, 4, 128), BF)
    held[5] = vm((256, 128), BF)
    msa, pair = pl.pallas_call(
        body,
        out_shape=(pltpu.VMEM((512, 128), BF), pltpu.VMEM((256, 128), BF)),
        in_specs=[pl.BlockSpec(memory_space=pltpu.HBM)] * len(operands),
        out_specs=[pl.BlockSpec(memory_space=pltpu.VMEM)] * 2,
        scratch_shapes=held
        + [
            vm((1024, 128), F32),
            vm((4, 256, 128), BF),
            vm((128, 1024), BF),
            vm((4, 8, 32, 256), BF),
            vm((4, 320, 128), BF),
            vm((8, 128, 256), BF),
            vm((8, 32, 256), F32),
            vm((8, 32, 256), F32),
            vm((32, 8, 256), BF),
            vm((32, 8, 256), BF),
            vm((8, 256), BF),
            vm((32, 8, 256), BF),
            vm((16, 8, 256), BF),
            vm((4, 32, 8, 256), BF),
            vm((32, 2, 8, 256), BF),
            vm((2, 256, 256), BF),
            vm((64, 256), F32),
            vm((256, 64), BF),
            vm((2, 4, 256, 128), BF),
            vm((8, 4, 2, 32, 128), BF),
            vm((64, 4096), BF),
            vm((4, 1024, 256), BF),
            vm((4, 8, 32, 128), BF),
            vm((4, 8, 32, 128), BF),
            vm((32, 8, 128), BF),
            vm((32, 8, 128), BF),
            vm((8, 32, 128), BF),
            vm((4, 2, 32, 128), BF),
            vm((4, 2, 32, 128), BF),
            vm((8, 32, 128), BF),
            vm((2, 2, 256, 128), BF),
            vm((32, 2, 8, 128), BF),
            vm((2, 32, 8, 128), BF),
            pltpu.SemaphoreType.DMA((17,)),
            pltpu.SemaphoreType.DMA((54,)),
            pltpu.SemaphoreType.DMA((54,)),
        ],
        compiler_params=pltpu.CompilerParams(
            collective_id=0, has_side_effects=True, vmem_limit_bytes=48 * 2**20
        ),
    )(*(pltpu.with_memory_space_constraint(x, pltpu.HBM) for x in operands))
    msa, pair = pl.pallas_call(
        hand_over,
        out_shape=(
            jax.ShapeDtypeStruct((512, 128), BF),
            jax.ShapeDtypeStruct((256, 128), BF),
        ),
        in_specs=[pl.BlockSpec(memory_space=pltpu.VMEM)] * 2,
        out_specs=[pl.BlockSpec(memory_space=pltpu.HBM)] * 2,
        scratch_shapes=[pltpu.SemaphoreType.DMA((2,))],
    )(*(pltpu.with_memory_space_constraint(x, pltpu.VMEM) for x in (msa, pair)))
    return msa.reshape(64, 8, 128), pair.reshape(32, 8, 128)


def solution(mesh):
    return jax.shard_map(
        shards,
        mesh=mesh,
        in_specs=(
            P("seq", "row", None),
            P("seq", "row", None),
            P(),
            P(),
            P(),
            P(),
            P(),
            P(),
            P(),
            P(),
            P(None, "seq", None),
            P("seq", None),
            P("seq"),
            P(None, "seq"),
            P(),
            P("seq", None),
            P(None, "seq"),
        ),
        out_specs=(P("seq", "row", "branch"), P("seq", "row", "branch")),
        check_vma=False,
    )
```

```python
import jax
import jax.numpy as jnp
from jax import lax
from jax.experimental import pallas as pl
from jax.experimental.pallas import tpu as pltpu
from jax.sharding import PartitionSpec as P

EPSILON = 1e-05
BF = jnp.bfloat16
F32 = jnp.float32
NZ, NW = 8, 4
NR = NZ * NW
NQ = 4


def mm(a, b):
    return jnp.dot(a, b, preferred_element_type=F32)


def mm_t(a, b):
    return lax.dot_general(a, b, (((1,), (1,)), ((), ())), preferred_element_type=F32)


def normalize(x, axis):
    average = jnp.mean(x, axis=axis, keepdims=True)
    centred = x - average
    spread = jnp.mean(centred * centred, axis=axis, keepdims=True)
    return centred * lax.rsqrt(spread + EPSILON)


def column(row):
    n = row.shape[1]
    eye = lax.broadcasted_iota(jnp.int32, (n, n), 0) == lax.broadcasted_iota(
        jnp.int32, (n, n), 1
    )
    return jnp.sum(jnp.where(eye, row, 0.0), axis=1, keepdims=True)


def body(
    a_hbm,
    p_hbm,
    ag_hbm,
    pg_hbm,
    aw_hbm,
    mw_hbm,
    oi_hbm,
    oo_hbm,
    bm_hbm,
    cg_hbm,
    ti_hbm,
    tg_hbm,
    tn_hbm,
    to_hbm,
    cn_hbm,
    up_hbm,
    dn_hbm,
    msa_ref,
    pair_ref,
    a_ref,
    p_ref,
    ag_ref,
    pg_ref,
    aw_ref,
    mw_ref,
    oi_ref,
    oo_ref,
    bm_ref,
    cg_ref,
    ti_ref,
    tg_ref,
    tn_ref,
    to_ref,
    cn_ref,
    up_ref,
    dn_ref,
    awf,
    awt,
    oot,
    g,
    w,
    tin,
    lt,
    rt,
    ls,
    rs,
    bs,
    lb,
    rb,
    bf,
    mn,
    nm,
    lx,
    lxt,
    qkv,
    rg,
    rgt,
    pq,
    ob,
    orb,
    tb,
    bk,
    xs,
    xr,
    pn,
    fb,
    mx,
    ao,
    mo,
    cs,
    ss,
    rv,
):
    b = lax.axis_index("branch")
    r = lax.axis_index("row")
    q = lax.axis_index("seq")
    zi = r // NW
    wi = r % NW
    inside = (r // (NR // 2)) == b
    cols = pl.ds(pl.multiple_of(b * 128, 128), 128)

    def signal(where):
        pl.semaphore_signal(
            barrier, inc=1, device_id=where, device_id_type=pl.DeviceIdType.MESH
        )

    def send(src, dst, k, where):
        pltpu.make_async_remote_copy(
            src_ref=src,
            dst_ref=dst,
            send_sem=ss.at[k],
            recv_sem=rv.at[k],
            device_id=where,
            device_id_type=pl.DeviceIdType.MESH,
        ).start()

    def arrived(view, k):
        pltpu.make_async_copy(view, view, rv.at[k]).wait()

    def left_here(view, k):
        pltpu.make_async_copy(view, view, ss.at[k]).wait()

    right_nb = {"seq": lax.rem(q + 1, NQ)}
    left_nb = {"seq": lax.rem(q + NQ - 1, NQ)}
    q_right = lax.rem(q + 1, NQ)
    q_left = lax.rem(q + NQ - 1, NQ)

    def both_ways(view, k):
        for c in range(2):
            send(view(q, c), view(q, c), k + c, right_nb)
            send(view(q, c), view(q, c), k + 2 + c, left_nb)

    def pass_on(view, k):
        arrived(view(q, 0), k)
        send(view(q_left, 0), view(q_left, 0), k + 4, right_nb)
        arrived(view(q, 1), k + 3)
        send(view(q_right, 1), view(q_right, 1), k + 5, left_nb)

    def g_part(slot, c):
        return g.at[slot, pl.ds(4 * c, 4)]

    def w_part(slot, c):
        return w.at[slot, pl.ds(160 * c, 160)]

    def row_peers(do):
        for dz in (4, 3, 5, 2, 6, 1, 7, 0):
            for dw in (2, 3, 1, 0):
                if dz or dw:
                    do(lax.rem(zi + dz, NZ) * NW + lax.rem(wi + dw, NW))

    loads = {}
    for n, (src, dst) in enumerate(
        (
            (p_hbm, p_ref),
            (a_hbm, a_ref),
            (tg_hbm, tg_ref),
            (tn_hbm, tn_ref),
            (to_hbm, to_ref),
            (up_hbm, up_ref),
            (dn_hbm, dn_ref),
            (pg_hbm, pg_ref),
            (oi_hbm, oi_ref),
            (aw_hbm.at[:, :, cols], aw_ref),
            (oo_hbm, oo_ref),
            (bm_hbm, bm_ref),
            (cg_hbm, cg_ref),
            (ti_hbm, ti_ref),
            (ag_hbm, ag_ref),
            (cn_hbm, cn_ref),
            (mw_hbm.at[:, cols], mw_ref),
        )
    ):
        loads[n] = pltpu.make_async_copy(src, dst, cs.at[n])
    loads[0].start()
    barrier = pltpu.get_barrier_semaphore()
    row_peers(lambda peer: signal({"row": peer}))
    for k in range(1, NQ):
        signal({"seq": lax.rem(q + k, NQ)})
    signal({"branch": 1 - b})
    for n in range(1, len(loads)):
        loads[n].start()

    loads[0].wait()
    g[q] = jnp.transpose(p_ref[...].astype(F32), (1, 0, 2)).astype(BF)
    loads[1].wait()

    pl.semaphore_wait(barrier, NR - 1 + NQ - 1 + 1)

    both_ways(g_part, 0)
    row_peers(lambda peer: send(a_ref.at[:, peer], mn.at[r], 12, {"row": peer}))

    for s in range(2):
        mn[r, s] = a_ref[s, r]
    for n in range(2, 7):
        loads[n].wait()
    w[q, 0:32] = tg_ref[...]
    w[q, 32:64] = (to_ref[...].astype(F32) * column(tn_ref[...])).astype(BF)
    w[q, 64:192] = up_ref[...]
    w[q, 192:320] = dn_ref[...]
    pass_on(g_part, 0)
    loads[7].wait()
    loads[8].wait()
    lane = lax.broadcasted_iota(jnp.int32, (16, 8, 256), 2) // 32
    sub = lax.broadcasted_iota(jnp.int32, (16, 8, 256), 1)
    wide_left = jnp.concatenate([oi_ref[0]] * 8, axis=0)
    for s in range(2):
        for k in range(2):
            x = a_ref[s, 16 * k : 16 * k + 16].astype(F32).reshape(128, 256)
            x = (normalize(x, 1) * pg_ref[...]).astype(BF)
            x = mm_t(x, wide_left).reshape(16, 8, 256)
            lx[32 * s + 16 * k : 32 * s + 16 * k + 16] = jnp.sum(
                jnp.where(lane == sub, x, 0.0), axis=1
            )
    lxt[...] = jnp.transpose(lx[...]).astype(BF)
    loads[9].wait()
    awf[0:1024] = aw_ref[...].astype(F32).reshape(1024, 128)
    for t in range(4):
        awt[t] = awf[pl.ds(t, 256, stride=4)].astype(BF)
    loads[10].wait()
    x = jnp.transpose(oo_ref[...].astype(F32), (1, 0, 2)).reshape(1024, 128)
    oot[...] = jnp.transpose(x).astype(BF)
    for n in range(11, 17):
        loads[n].wait()

    head_row = lax.broadcasted_iota(jnp.int32, (8, 128), 0)
    pick = jnp.where(head_row == NQ * b + q, bm_ref[...].astype(F32), 0.0)
    pick = jnp.sum(pick, axis=0, keepdims=True)
    pair_gain = column(cg_ref[...])

    def bias_row(i, acc):
        unit = normalize(g[:, i].astype(F32).reshape(128, 256), 0)
        tin[i] = (unit * pair_gain).astype(BF)
        return acc + mm(jnp.where(head_row == i, pick, 0.0).astype(BF), unit.astype(BF))

    arrived(g_part(q, 0), 2)
    arrived(g_part(q, 0), 4)
    acc = lax.fori_loop(0, 4, bias_row, jnp.zeros((8, 256), F32), unroll=4)
    arrived(g_part(q, 1), 1)
    arrived(g_part(q, 1), 5)
    bs[...] = lax.fori_loop(4, 8, bias_row, acc, unroll=4).astype(BF)
    bf[q, r] = bs[...]
    for dz in (4, 3, 5, 2, 6, 1, 7, 0):
        for dw in (2, 3, 1, 0):
            if dz or dw:
                peer = lax.rem(zi + dz, NZ) * NW + lax.rem(wi + dw, NW)
                send(bs, bf.at[q, r], 13 + dz, {"row": peer})
    def tri_row_step(i, carry):
        lin = mm(ti_ref[...].reshape(128, 128), tin[i])
        lt[i] = lin[0:32] * jax.nn.sigmoid(lin[32:64])
        rt[i] = lin[64:96] * jax.nn.sigmoid(lin[96:128])
        return carry

    lax.fori_loop(0, 8, tri_row_step, 0, unroll=4)
    ls[...] = jnp.transpose(lt[...], (1, 0, 2)).astype(BF)
    rs[...] = jnp.transpose(rt[...], (1, 0, 2)).astype(BF)
    lb[r] = ls[r]
    row_peers(lambda peer: send(ls.at[peer], lb.at[r], 33, {"row": peer}))

    @pl.when(inside)
    def _():
        rb[r % (NR // 2)] = rs[r]
        row_peers(lambda peer: send(rs.at[peer], rb.at[r % (NR // 2)], 34, {"row": peer}))

    both_ways(w_part, 6)

    arrived(mn.at[pl.ds(0, NR - 1)], 12)
    for s in range(2):
        x = normalize(mn[:, s].astype(F32).reshape(256, 256), 1)
        right = mm_t(oi_ref[1], (x * pg_ref[...]).astype(BF))
        rg[zi, wi, s] = jnp.where(b == 0, right[:, :128], right[:, 128:]).astype(BF)
        nm[s] = (x * ag_ref[...]).astype(BF)

    for k in (1, 7, 2, 6, 3, 5, 4):
        peer = {"row": lax.rem(zi + k, NZ) * NW + wi}
        send(rg.at[zi, wi], rg.at[zi, wi], 46 + k, peer)
    pass_on(w_part, 6)
    for s in range(2):
        qkv[s, 0] = (mm(nm[s], awt[0]) * (32.0**-0.5)).astype(BF)
        qkv[s, 1] = mm(nm[s], awt[1]).astype(BF)
        qkv[s, 2] = mm(nm[s], awt[2]).astype(BF)
        qkv[s, 3] = jax.nn.sigmoid(mm(nm[s], awt[3])).astype(BF)

    def group(slot, dz):
        return bf.at[slot, pl.ds(lax.rem(zi + NZ - dz, NZ) * NW, NW)]

    for dz in (0, 1, 7, 2, 6, 3, 5, 4):
        arrived(bf.at[0, pl.ds(0, NW if dz else NW - 1)], 13 + dz)
        part = group(q, dz)
        send(part, part, 31 if dz < 4 else 32, {"seq": lax.rem(q + 2, NQ)})
        send(part, part, 21 + dz if dz < 4 else 25, right_nb)
        send(part, part, 33 - dz if dz >= 4 else 30, left_nb)
    w_core = wi + 1 - 2 * (wi % 2)
    w_far = lax.rem(wi + 2, NW)
    other_core = {"row": zi * NW + w_core}
    near, rest = (0, 1, 7, 2, 6), (3, 5, 4)

    def onward(distances, slot, k, where):
        for dz in distances:
            block = rg.at[lax.rem(zi + NZ - dz, NZ), slot]
            send(block, block, k, where)

    def from_z(distances, k):
        for dz in distances:
            if dz:
                arrived(rg.at[0, 0], 46 + dz)
            onward((dz,), wi, k, {"row": zi * NW + w_far})
            onward((dz,), wi, 36, other_core)

    from_z(near, 37)
    from_z(rest, 35)

    arrived(lb.at[pl.ds(0, NR - 1)], 33)

    @pl.when(inside)
    def _():
        arrived(rb.at[pl.ds(0, NR // 2 - 1)], 34)

    @pl.when(jnp.logical_not(inside))
    def _():
        arrived(rb, 34)

    tl = lb[...].astype(F32).reshape(256, 256).astype(BF)
    tr = rb[...].astype(F32).reshape(128, 256).astype(BF)
    tb[...] = mm_t(tl, tr).reshape(32, 8, 128).astype(BF)
    bk[r] = tb[r]
    row_peers(lambda peer: send(tb.at[peer], bk.at[r], 39, {"row": peer}))

    lane_head = lax.broadcasted_iota(jnp.int32, (256, 128), 1) // 32
    for s in range(2):
        value = jnp.zeros((256, 128), F32)
        for k in range(NQ):
            h = lax.rem(q + (0, 1, 3, 2)[k], NQ)
            if s == 0 and k == 1:
                arrived(bf.at[0, pl.ds(0, 4 * NW)], 30)
                for n in range(4):
                    arrived(bf.at[0, pl.ds(0, NW)], 26 + n)
            if s == 0 and k == 2:
                arrived(bf.at[0, pl.ds(0, 4 * NW)], 25)
                for n in range(4):
                    arrived(bf.at[0, pl.ds(0, NW)], 21 + n)
            if s == 0 and k == 3:
                arrived(bf.at[0, pl.ds(0, 4 * NW)], 31)
                arrived(bf.at[0, pl.ds(0, 4 * NW)], 32)
            here = lane_head == h
            query = jnp.where(here, qkv[s, 0].astype(F32), 0.0).astype(BF)
            score = mm_t(query, qkv[s, 1]) + bf[h].astype(F32).reshape(256, 256)
            expo = jnp.exp(score - jnp.max(score, axis=1, keepdims=True))
            total = jnp.sum(expo, axis=1, keepdims=True)
            value = jnp.where(here, mm(expo.astype(BF), qkv[s, 2]) / total, value)
        mx[b, s] = (qkv[s, 3].astype(F32) * value).astype(BF)
        send(mx.at[b, s], mx.at[b, s], 43 + s, {"branch": 1 - b})

    arrived(rg.at[pl.ds(0, 5), 0], 37)
    onward(near, w_far, 38, other_core)
    arrived(rg.at[pl.ds(0, 3), 0], 35)
    onward(rest, w_far, 38, other_core)

    arrived(rg.at[:, 0], 36)
    arrived(rg.at[:, 0], 38)
    for s in range(2):
        x = rg[:, :, s].astype(F32).reshape(32, 32, 128)
        x = jnp.transpose(x, (1, 0, 2)).astype(BF)
        for d in range(32):
            rgt[32 * s : 32 * s + 32, 128 * d : 128 * d + 128] = x[d]

    for s in range(2):
        arrived(mx.at[0, s], 43 + s)
        x = mm(mx[0, s], mw_ref[0:128]) + mm(mx[1, s], mw_ref[128:256])
        x = mn[:, s, :, cols].astype(F32).reshape(256, 128) + x
        ao[:, s] = x.reshape(32, 8, 128).astype(BF)
        mo[s, r] = ao[r, s]
        row_peers(lambda peer: send(ao.at[peer, s], mo.at[s, r], 45 + s, {"row": peer}))

    arrived(bk.at[pl.ds(0, NR - 1)], 39)
    xs[...] = jnp.transpose(bk[...].astype(F32), (1, 0, 2)).astype(BF)
    xr[q] = xs[pl.ds(2 * q, 2)]
    for k in (2, 1, 3):
        peer = lax.rem(q + k, NQ)
        send(xs.at[pl.ds(2 * peer, 2)], xr.at[q], 40, {"seq": peer})

    def outer_step(n, carry):
        x = mm(lxt[...], rgt[:, pl.ds(pl.multiple_of(n * 256, 256), 256)]).astype(BF)
        for d in range(2):
            for i in range(8):
                pq[
                    i // 2,
                    pl.ds(pl.multiple_of(n * 64 + 32 * d, 32), 32),
                    128 * (i % 2) : 128 * (i % 2) + 128,
                ] = x[32 * i : 32 * i + 32, 128 * d : 128 * d + 128]
        return carry

    lax.fori_loop(0, 16, outer_step, 0, unroll=8)

    for n in range(4):
        x = (mm(oot[...], pq[n]) * (1.0 / 256.0)).astype(BF)
        for i in range(2):
            ob[:, 2 * n + i] = x[:, 128 * i : 128 * i + 128].reshape(4, 32, 128)
    orb[q] = ob[q]
    for k in (2, 1, 3):
        peer = lax.rem(q + k, NQ)
        send(ob.at[peer], orb.at[q], 42, {"seq": peer})

    for k, c in ((7, 1), (8, 0), (10, 0), (11, 1)):
        arrived(w_part(q, c), k)
    out_w = w[:, 32:64].astype(F32).reshape(128, 128)
    out_w = jnp.transpose(out_w).astype(BF)
    trans_gain = column(cn_ref[...])
    pair_in = jnp.concatenate(
        [g[:, 2 * q + i, :, cols].astype(F32).reshape(128, 128) for i in range(2)], axis=1
    )
    tri_row = jnp.concatenate([tin[2 * q + i, :, cols] for i in range(2)], axis=1)
    gate = jax.nn.sigmoid(mm(w[:, 0:32].reshape(128, 128), tri_row))
    arrived(xr.at[pl.ds(0, NQ - 1)], 40)
    row_tri = jnp.concatenate(
        [xr[:, i].astype(F32).reshape(128, 128) for i in range(2)], axis=1
    )
    first = pair_in + gate * mm(out_w, normalize(row_tri, 0).astype(BF))
    first = first.astype(BF).astype(F32)
    trans = (normalize(first, 0) * trans_gain).astype(BF)
    moved = first
    for k in range(NQ):
        hidden = jnp.maximum(mm(w[k, 64:192], trans), 0.0).astype(BF)
        moved = moved + mm(w[k, 192:320], hidden)
    moved = moved.astype(BF)
    for i in range(2):
        pn[:, i] = moved[:, 128 * i : 128 * i + 128].reshape(4, 32, 128)
    fb[pl.ds(2 * q, 2)] = pn[q]
    for k in (2, 1, 3):
        peer = lax.rem(q + k, NQ)
        send(pn.at[peer], fb.at[pl.ds(2 * q, 2)], 41, {"seq": peer})

    for c in range(2):
        for k in (0, 2, 4):
            left_here(g_part(q, c), k + c)
            left_here(w_part(q, c), 6 + k + c)
    for n in range(8):
        left_here(bf.at[0, pl.ds(0, NW if n else NW - 1)], 13 + n)
    for n in range(1, NZ):
        left_here(rg.at[0, 0], 46 + n)
    for n in range(4):
        left_here(bf.at[0, pl.ds(0, NW)], 21 + n)
        left_here(bf.at[0, pl.ds(0, NW)], 26 + n)
    for k in (25, 30, 31, 32):
        left_here(bf.at[0, pl.ds(0, 4 * NW)], k)
    for k, view in (
        (12, mn.at[pl.ds(0, NR - 1)]),
        (33, lb.at[pl.ds(0, NR - 1)]),
        (35, rg.at[pl.ds(0, 3), 0]),
        (36, rg.at[:, 0]),
        (37, rg.at[pl.ds(0, 5), 0]),
        (38, rg.at[:, 0]),
        (39, bk.at[pl.ds(0, NR - 1)]),
        (40, xr.at[pl.ds(0, NQ - 1)]),
        (43, mx.at[0, 0]),
        (44, mx.at[0, 0]),
    ):
        left_here(view, k)

    @pl.when(inside)
    def _():
        left_here(lb.at[pl.ds(0, NR - 1)], 34)

    arrived(orb.at[pl.ds(0, NQ - 1)], 42)
    update = orb[0].astype(F32)
    for k in range(1, NQ):
        update = update + orb[k].astype(F32)
    update = update.astype(BF).astype(F32)
    arrived(fb.at[pl.ds(0, 6)], 41)
    update = update + fb[...].astype(F32)
    pair_ref[...] = jnp.transpose(update, (1, 0, 2)).reshape(256, 128).astype(BF)

    for s in range(2):
        arrived(mo.at[s, pl.ds(0, NR - 1)], 45 + s)
        msa_ref[256 * s : 256 * s + 256] = mo[s].astype(F32).reshape(256, 128).astype(BF)

    left_here(fb.at[pl.ds(0, 6)], 41)
    left_here(orb.at[pl.ds(0, NQ - 1)], 42)
    for s in range(2):
        left_here(mo.at[0, pl.ds(0, NR - 1)], 45 + s)


def hand_over(msa_in, pair_in, msa_out, pair_out, sems):
    copies = (
        pltpu.make_async_copy(msa_in, msa_out, sems.at[0]),
        pltpu.make_async_copy(pair_in, pair_out, sems.at[1]),
    )
    for copy in copies:
        copy.start()
    for copy in copies:
        copy.wait()


def shards(
    alignment_input,
    pairwise_input,
    alignment_gain,
    product_gain,
    attention_weight,
    mixing_weight,
    outer_input_weight,
    outer_output_weight,
    bias_matrix,
    pairwise_gain,
    triangle_input_weight,
    triangle_gate_weight,
    triangle_gain,
    triangle_output_weight,
    transition_gain,
    transition_up_weight,
    transition_down_weight,
):
    operands = (
        alignment_input.reshape(2, NR, 8, 256),
        pairwise_input,
        alignment_gain.reshape(1, 256),
        product_gain.reshape(1, 256),
        attention_weight,
        mixing_weight,
        outer_input_weight.transpose(1, 2, 0),
        outer_output_weight,
        bias_matrix.T,
        pairwise_gain.reshape(1, 128),
        triangle_input_weight,
        triangle_gate_weight,
        triangle_gain.reshape(1, 32),
        triangle_output_weight.T,
        transition_gain.reshape(1, 128),
        transition_up_weight,
        transition_down_weight,
    )
    vm = pltpu.VMEM
    held = [vm(x.shape, x.dtype) for x in operands]
    held[4] = vm((256, 4, 128), BF)
    held[5] = vm((256, 128), BF)
    msa, pair = pl.pallas_call(
        body,
        out_shape=(pltpu.VMEM((512, 128), BF), pltpu.VMEM((256, 128), BF)),
        in_specs=[pl.BlockSpec(memory_space=pltpu.HBM)] * len(operands),
        out_specs=[pl.BlockSpec(memory_space=pltpu.VMEM)] * 2,
        scratch_shapes=held
        + [
            vm((1040, 128), F32),
            vm((4, 256, 128), BF),
            vm((128, 1024), BF),
            vm((4, 8, 32, 256), BF),
            vm((4, 320, 128), BF),
            vm((8, 128, 256), BF),
            vm((8, 32, 256), F32),
            vm((8, 32, 256), F32),
            vm((32, 8, 256), BF),
            vm((32, 8, 256), BF),
            vm((8, 256), BF),
            vm((32, 8, 256), BF),
            vm((16, 8, 256), BF),
            vm((4, 32, 8, 256), BF),
            vm((32, 2, 8, 256), BF),
            vm((2, 256, 256), BF),
            vm((64, 256), F32),
            vm((256, 64), BF),
            vm((2, 4, 256, 128), BF),
            vm((8, 4, 2, 32, 128), BF),
            vm((64, 4096), BF),
            vm((4, 1024, 256), BF),
            vm((4, 8, 32, 128), BF),
            vm((4, 8, 32, 128), BF),
            vm((32, 8, 128), BF),
            vm((32, 8, 128), BF),
            vm((8, 32, 128), BF),
            vm((4, 2, 32, 128), BF),
            vm((4, 2, 32, 128), BF),
            vm((8, 32, 128), BF),
            vm((2, 2, 256, 128), BF),
            vm((32, 2, 8, 128), BF),
            vm((2, 32, 8, 128), BF),
            pltpu.SemaphoreType.DMA((17,)),
            pltpu.SemaphoreType.DMA((54,)),
            pltpu.SemaphoreType.DMA((54,)),
        ],
        compiler_params=pltpu.CompilerParams(
            collective_id=0, has_side_effects=True, vmem_limit_bytes=48 * 2**20
        ),
    )(*(pltpu.with_memory_space_constraint(x, pltpu.HBM) for x in operands))
    msa, pair = pl.pallas_call(
        hand_over,
        out_shape=(
            jax.ShapeDtypeStruct((512, 128), BF),
            jax.ShapeDtypeStruct((256, 128), BF),
        ),
        in_specs=[pl.BlockSpec(memory_space=pltpu.VMEM)] * 2,
        out_specs=[pl.BlockSpec(memory_space=pltpu.HBM)] * 2,
        scratch_shapes=[pltpu.SemaphoreType.DMA((2,))],
    )(*(pltpu.with_memory_space_constraint(x, pltpu.VMEM) for x in (msa, pair)))
    return msa.reshape(64, 8, 128), pair.reshape(32, 8, 128)


def solution(mesh):
    return jax.shard_map(
        shards,
        mesh=mesh,
        in_specs=(
            P("seq", "row", None),
            P("seq", "row", None),
            P(),
            P(),
            P(),
            P(),
            P(),
            P(),
            P(),
            P(),
            P(None, "seq", None),
            P("seq", None),
            P("seq"),
            P(None, "seq"),
            P(),
            P("seq", None),
            P(None, "seq"),
        ),
        out_specs=(P("seq", "row", "branch"), P("seq", "row", "branch")),
        check_vma=False,
    )
```
